32 devices in a mesh: row: 4 (over y, core), col: 8 (over z, x).
Axes of the slice: x: 2, y: 2, z: 4, core: 2. Of those that a mesh axis runs over, the one named last changes fastest.
Arguments:
- inputs: bfloat16 [512, 8192], P('row', 'col'), may hold values from -6 to 6
- grad_out: bfloat16 [512, 8192], P('row', 'col'), may hold values from -1.5 to 1.5
- up_blocks: bfloat16 [8, 1024, 128], P('row', 'col'), may hold values from -0.5 to 0.5
- up_where: int32 [8, 16], P('row', 'col'), may hold values from -1 to 47, as said below
- down_blocks: bfloat16 [8, 1024, 128], P('row', 'col'), may hold values from -0.5 to 0.5
- down_where: int32 [8, 16], P('row', 'col'), may hold values from -1 to 47, as said below
Outputs:
- grad_in: bfloat16 [512, 8192], P('row', 'col')
- up_grad: bfloat16 [8, 1024, 128], P('row', 'col')
- down_grad: bfloat16 [8, 1024, 128], P('row', 'col')
The draws below stay inside these ranges and needn't reach their ends.
Inputs may be any that keep to these rules, and one draw needn't show every extreme that they name: `up_where`: each grid owner (r, c) has 2 slots; a used slot names a block row below 16 and a block column below 48 of the owner's part of W1, used slots of one owner name distinct blocks and come first, unused slots hold -1 in both entries. In some grid column every owner uses all 2 slots, and some owner leaves a slot unused. `down_where`: as for up_where, with the first entry a hidden block below 48 and the second a model-width block below 16 of the owner's part of W2.
All inputs are finite; a program needn't handle non-finite values.
Results may differ from the reference program's by a relative error of at most 0.013.
Values may be sent and summed in bfloat16 or wider, within the bound.
A program may use at most 64 MiB of HBM per device.

```python
import jax
import jax.numpy as jnp
from jax import lax

D = 8192
BLK = 128
SLOTS = 2
TOK_DEV = 128
TOKENS = 512
RB = 16
CB = 48
N_ROW = 4
N_COL = 8


def layout_draw(key, first_span, second_span):
    owners = N_ROW * N_COL
    spots = first_span * second_span
    key_order, key_count, key_full = jax.random.split(key, 3)
    scores = jax.random.randint(key_order, (owners, spots), 0, 1 << 20) * spots + jnp.arange(spots, dtype=jnp.int32)[None, :]
    full_col = jax.random.randint(key_full, (), 0, N_COL)
    owner_ids = jnp.arange(owners, dtype=jnp.int32)
    spot_ids = jnp.arange(spots, dtype=jnp.int32)
    corner = (owner_ids[:, None] == full_col) & (spot_ids[None, :] == spots - 1)
    scores = jnp.where(corner, -1, scores)
    chosen = jnp.argsort(scores, axis=1)[:, :SLOTS].astype(jnp.int32)
    counts = jax.random.randint(key_count, (owners,), 0, SLOTS + 1)
    owner_col = owner_ids % N_COL
    counts = jnp.where(owner_col == full_col, SLOTS, counts)
    short_owner = (full_col + 1) % N_COL
    counts = jnp.where(owner_ids == short_owner, SLOTS - 1, counts)
    used = jnp.arange(SLOTS, dtype=jnp.int32)[None, :] < counts[:, None]
    first = jnp.where(used, chosen // second_span, -1)
    second = jnp.where(used, chosen % second_span, -1)
    pairs = jnp.stack([first, second], axis=-1).astype(jnp.int32)
    pairs = pairs.reshape(N_ROW, N_COL, SLOTS, 2)
    pairs = jnp.transpose(pairs, (0, 2, 1, 3))
    return pairs.reshape(N_ROW * SLOTS, N_COL * 2)


def draw_up_where(key, part):
    return layout_draw(jax.random.fold_in(key, 11), RB, CB)


def draw_down_where(key, part):
    return layout_draw(jax.random.fold_in(key, 23), CB, RB)


def levels(own_key, dims, pieces, least, top_value):
    gain, own = 1.0, jax.random.fold_in(own_key, 6)
    for axis_at, blocks in pieces:
        steps = jnp.exp(jax.random.uniform(jax.random.fold_in(own, axis_at), (blocks,), jnp.float32, least / len(pieces), top_value / len(pieces)))
        gain = gain * jnp.repeat(steps, dims[axis_at] // blocks).reshape([-1 if axis == axis_at else 1 for axis in range(len(dims))])
    return gain


def bell_draw(key, shape, scale, bound, pieces=(), kind=jnp.bfloat16):
    drawn = scale * jax.random.normal(key, shape, jnp.float32)
    if pieces:
        drawn = drawn * levels(key, shape, pieces, -0.22, 0.18)
    return jnp.clip(drawn, -bound, bound).astype(kind)


def setup_inputs(seed: int = 0) -> dict:
    splits = jax.random.split(jax.random.key(seed), 7)
    return {
        "inputs": bell_draw(splits[0], (TOKENS, D), 1.0, 6.0, ((0, 4), (1, 8))),
        "grad_out": bell_draw(splits[1], (TOKENS, D), 0.25, 1.5, ((0, 4), (1, 8))),
        "up_blocks": bell_draw(splits[2], (N_ROW * SLOTS, N_COL * BLK, BLK), BLK ** -0.5, 0.5, ((0, 4), (1, 8))),
        "up_where": draw_up_where(jax.random.fold_in(splits[6], 71), 0),
        "down_blocks": bell_draw(splits[4], (N_ROW * SLOTS, N_COL * BLK, BLK), BLK ** -0.5, 0.5, ((0, 4), (1, 8))),
        "down_where": draw_down_where(jax.random.fold_in(splits[6], 71), 0),
    }


def gelu_parts(hidden):
    cube = hidden * hidden * hidden
    inner = 0.7978845608028654 * (hidden + 0.044715 * cube)
    tanh_val = jnp.tanh(inner)
    value = 0.5 * hidden * (1.0 + tanh_val)
    slope = 0.5 * (1.0 + tanh_val) + 0.5 * hidden * (1.0 - tanh_val * tanh_val) * 0.7978845608028654 * (1.0 + 0.134145 * hidden * hidden)
    return value, slope


def to_bf16_f32(values):
    rounded = lax.optimization_barrier(values.astype(jnp.bfloat16))
    return rounded.astype(jnp.float32)


def reference(inputs, grad_out, up_blocks, up_where, down_blocks, down_where):
    all_slots = N_ROW * SLOTS
    d_count = D // BLK
    owner_idx = jnp.arange(all_slots, dtype=jnp.int32) // SLOTS
    rows_in = inputs.astype(jnp.float32).reshape(TOKENS, d_count, BLK)
    rows_grad = grad_out.astype(jnp.float32).reshape(TOKENS, d_count, BLK)

    def column_work(carry, column):
        up_mat = lax.dynamic_slice_in_dim(up_blocks, column * BLK, BLK, 1).astype(jnp.float32)
        up_pos = lax.dynamic_slice_in_dim(up_where, column * 2, 2, 1)
        down_mat = lax.dynamic_slice_in_dim(down_blocks, column * BLK, BLK, 1).astype(jnp.float32)
        down_pos = lax.dynamic_slice_in_dim(down_where, column * 2, 2, 1)
        up_valid = up_pos[:, 1] >= 0
        up_row = jnp.where(up_valid, owner_idx * RB + up_pos[:, 0], 0).astype(jnp.int32)
        up_col = jnp.where(up_valid, up_pos[:, 1], 0).astype(jnp.int32)
        up_mat = jnp.where(up_valid[:, None, None], up_mat, jnp.zeros_like(up_mat))
        down_valid = down_pos[:, 0] >= 0
        down_frow = jnp.where(down_valid, down_pos[:, 0], 0).astype(jnp.int32)
        down_dcol = jnp.where(down_valid, owner_idx * RB + down_pos[:, 1], 0).astype(jnp.int32)
        down_mat = jnp.where(down_valid[:, None, None], down_mat, jnp.zeros_like(down_mat))
        x_sel = jnp.take(rows_in, up_row, axis=1)
        y_sel = jnp.take(rows_grad, down_dcol, axis=1)
        block_out = jnp.einsum('tsk,skj->tsj', x_sel, up_mat)
        hidden = jnp.zeros((TOKENS, CB, BLK), jnp.float32).at[:, up_col].add(block_out)
        value, slope = gelu_parts(hidden)
        act = to_bf16_f32(value)
        act_sel = jnp.take(act, down_frow, axis=1)
        down_terms = jnp.einsum('rtsf,rtsd->rsfd', act_sel.reshape(N_ROW, TOK_DEV, all_slots, BLK), y_sel.reshape(N_ROW, TOK_DEV, all_slots, BLK))
        down_sum = jnp.sum(to_bf16_f32(down_terms), axis=0)
        down_sum = jnp.where(down_valid[:, None, None], down_sum, jnp.zeros_like(down_sum)).astype(jnp.bfloat16)
        down_part = jnp.einsum('tsd,sfd->tsf', y_sel, down_mat)
        grad_act = jnp.zeros((TOKENS, CB, BLK), jnp.float32).at[:, down_frow].add(down_part)
        grad_hidden = to_bf16_f32(grad_act * slope)
        dh_sel = jnp.take(grad_hidden, up_col, axis=1)
        up_terms = jnp.einsum('rtsk,rtsj->rskj', x_sel.reshape(N_ROW, TOK_DEV, all_slots, BLK), dh_sel.reshape(N_ROW, TOK_DEV, all_slots, BLK))
        up_sum = jnp.sum(to_bf16_f32(up_terms), axis=0)
        up_sum = jnp.where(up_valid[:, None, None], up_sum, jnp.zeros_like(up_sum)).astype(jnp.bfloat16)
        back = jnp.einsum('tsj,skj->tsk', dh_sel, up_mat)
        partial_value = jnp.zeros((TOKENS, d_count, BLK), jnp.float32).at[:, up_row].add(back)
        partial_value = to_bf16_f32(partial_value.reshape(TOKENS, D))
        return carry + partial_value, (up_sum, down_sum)

    start = jnp.zeros((TOKENS, D), jnp.float32)
    summed, grads = lax.scan(column_work, start, jnp.arange(N_COL, dtype=jnp.int32))
    up_all, down_all = grads
    grad_in = summed.astype(jnp.bfloat16)
    up_grad = jnp.transpose(up_all, (1, 0, 2, 3)).reshape(all_slots, N_COL * BLK, BLK)
    down_grad = jnp.transpose(down_all, (1, 0, 2, 3)).reshape(all_slots, N_COL * BLK, BLK)
    return (grad_in, up_grad, down_grad)
```

```python
import functools

import jax
import jax.numpy as jnp
from jax import lax
from jax.experimental import pallas as pl
from jax.experimental.pallas import tpu as pltpu
from jax.sharding import PartitionSpec as P

MESH = pl.DeviceIdType.MESH
CHUNKS = 2


def gelu_parts(hidden):
    cube = hidden * hidden * hidden
    inner = 0.7978845608028654 * (hidden + 0.044715 * cube)
    tanh_val = jnp.tanh(inner)
    value = 0.5 * hidden * (1.0 + tanh_val)
    slope = 0.5 * (1.0 + tanh_val) + 0.5 * hidden * (
        1.0 - tanh_val * tanh_val
    ) * 0.7978845608028654 * (1.0 + 0.134145 * hidden * hidden)
    return (value, slope)


def dot(left, right, left_dim, right_dim):
    return lax.dot_general(
        left, right, (((left_dim,), (right_dim,)), ((), ())),
        preferred_element_type=jnp.float32,
    )


def flag(pred):
    return pred.astype(jnp.float32)


def kernel(
    rows, pairs, slots, chunks,
    x_hbm, y_hbm, up_hbm, dn_hbm, up_pos, dn_pos,
    gin_ref, ugrad_ref, dgrad_ref,
    own_pos, row_pos, grp_pos, row_tab, grp_tab,
    x_all, y_all, x_out, y_out, x_sel, y_sel,
    up_mat, dn_mat, block_out, down_part, act, dhid,
    back_out, back_in, fold_out, fold_in,
    up_out, up_in, dn_out, dn_in,
    loc_sem, own_sem, tab_sem,
    rp_send, rp_recv, gp_send, gp_recv, ex_send, ex_recv, w_send, w_recv,
    sel_send, sel_recv, bk_send, bk_recv, fx_send, fx_recv, gr_send, gr_recv,
):
    row = lax.axis_index("row")
    col = lax.axis_index("col")
    group, part = col // pairs, col % pairs
    tok = x_hbm.shape[0]
    blk = up_hbm.shape[1]
    wide = x_hbm.shape[1] // blk
    step = tok // chunks
    total = rows * slots

    def row_peer(k):
        return (lax.rem(row + k, rows), col)

    def grp_of(k):
        return lax.rem(group + k, rows)

    def grp_peer(k):
        return (row, grp_of(k) * pairs + part)

    def part_of(k):
        return lax.rem(part + k, pairs)

    def part_peer(k):
        return (row, group * pairs + part_of(k))

    def remote(src, dst, send, recv, peer):
        return pltpu.make_async_remote_copy(
            src_ref=src, dst_ref=dst, send_sem=send, recv_sem=recv,
            device_id=peer, device_id_type=MESH,
        )

    peers = [row_peer(k) for k in range(1, rows)]
    peers += [grp_peer(k) for k in range(1, rows)]
    peers += [part_peer(k) for k in range(1, pairs)]

    mine = pl.ds(row * slots, slots)
    loads = [
        pltpu.make_async_copy(up_hbm, up_mat.at[mine], loc_sem.at[2]),
        pltpu.make_async_copy(dn_hbm, dn_mat.at[mine], loc_sem.at[3]),
    ]
    for load in loads:
        load.start()
    home = pl.ds(part * wide, wide)
    for a, (src, dst) in enumerate(((x_hbm, x_all), (y_hbm, y_all))):
        for t in range(chunks):
            for b in range(wide):
                pltpu.make_async_copy(
                    src.at[pl.ds(t * step, step), pl.ds(b * blk, blk)],
                    dst[t].at[part * wide + b], own_sem.at[a, t],
                ).start()
            loads.append(
                pltpu.make_async_copy(dst[t].at[home], dst[t].at[home], own_sem.at[a, t])
            )
    lane = lax.broadcasted_iota(jnp.int32, (8, 128), 1)
    sub = lax.broadcasted_iota(jnp.int32, (8, 128), 0)
    packed = jnp.full((8, 128), -1, jnp.int32)
    for s in range(slots):
        for j, src in enumerate((up_pos, up_pos, dn_pos, dn_pos)):
            packed = jnp.where((sub == s) & (lane == j), src[s, j % 2], packed)
    own_pos[...] = packed
    row_pos[row] = packed

    barrier = pltpu.get_barrier_semaphore()
    for peer in peers:
        pl.semaphore_signal(barrier, inc=1, device_id=peer, device_id_type=MESH)
    pl.semaphore_wait(barrier, len(peers))

    pos_row = []
    for k in range(1, rows):
        copy = remote(own_pos, row_pos.at[row], rp_send.at[k], rp_recv.at[k], row_peer(k))
        copy.start()
        pos_row.append(copy)
    swap = {}
    for t in range(chunks):
        here = pl.ds(t * step, step)
        for a, (src, dst) in enumerate(((x_hbm, x_all), (y_hbm, y_all))):
            for k in range(1, pairs):
                sems = (ex_send.at[a, t, k], ex_recv.at[a, t, k], part_peer(k))
                for b in range(wide):
                    remote(
                        src.at[here, pl.ds(b * blk, blk)],
                        dst[t].at[part * wide + b], *sems,
                    ).start()
                swap[a, t, k] = remote(dst[t].at[home], dst[t].at[home], *sems)
    mats = []
    for a, (src, dst) in enumerate(((up_hbm, up_mat), (dn_hbm, dn_mat))):
        for k in range(1, rows):
            copy = remote(src, dst.at[mine], w_send.at[a, k], w_recv.at[a, k], row_peer(k))
            copy.start()
            mats.append(copy)

    for copy in pos_row:
        copy.wait()
    pos_grp = []
    for k in range(1, rows):
        copy = remote(
            row_pos.at[grp_of(k)], grp_pos.at[group],
            gp_send.at[k], gp_recv.at[k], grp_peer(k),
        )
        copy.start()
        pos_grp.append(copy)
    grp_pos[group] = row_pos[group]
    row_copy = pltpu.make_async_copy(row_pos, row_tab, tab_sem.at[0])
    row_copy.start()
    for copy in pos_grp:
        copy.wait()
    row_copy.wait()
    grp_copy = pltpu.make_async_copy(grp_pos, grp_tab, tab_sem.at[1])
    grp_copy.start()
    grp_copy.wait()
    for load in loads:
        load.wait()

    sel = {}
    for t in range(chunks):
        here = pl.ds(t * step, step)
        for a, (src, out, dst) in enumerate(((x_all, x_out, x_sel), (y_all, y_out, y_sel))):
            for k in range(1, pairs):
                swap[a, t, k].wait_recv()

            def pick(whose, s):
                return src[t][jnp.maximum(grp_tab[whose, s, 3 * a], 0)]

            for k in range(1, rows):
                for s in range(slots):
                    out[k, s, here] = pick(grp_of(k), s)
                copy = remote(
                    out.at[k, :, here], dst.at[pl.ds(group * slots, slots), here],
                    sel_send.at[a, t, k], sel_recv.at[a, t, k], grp_peer(k),
                )
                copy.start()
                sel[a, t, k] = copy
            for s in range(slots):
                dst[group * slots + s, here] = pick(group, s)

    for copy in mats:
        copy.wait_recv()

    def up_col(i):
        return row_tab[i // slots, i % slots, 1]

    def down_row(i):
        return row_tab[i // slots, i % slots, 2]

    back = {}
    for t in range(chunks):
        here = pl.ds(t * step, step)
        for a in range(2):
            for k in range(1, rows):
                sel[a, t, k].wait_recv()

        @pl.loop(0, total)
        def _(i):
            block_out[i] = dot(x_sel[i, here], up_mat[i], 1, 0)
            down_part[i] = dot(y_sel[i, here], dn_mat[i], 1, 1)

        @pl.loop(0, total)
        def _(i):
            spot = up_col(i)
            hidden = jnp.zeros((step, blk), jnp.float32)
            grad = jnp.zeros((step, blk), jnp.float32)
            for j in range(total):
                hidden += flag((up_col(j) == spot) & (spot >= 0)) * block_out[j]
                grad += flag((down_row(j) == spot) & (spot >= 0)) * down_part[j]
            _, slope = gelu_parts(hidden)
            dh = (grad * slope).astype(jnp.bfloat16)
            dhid[i, here] = dh
            back_out[i, here] = dot(dh, up_mat[i], 1, 1).astype(jnp.bfloat16)

        for k in range(1, rows):
            copy = remote(
                back_out.at[pl.ds(grp_of(k) * slots, slots), here],
                back_in.at[pl.ds(group * slots, slots), here],
                bk_send.at[t, k], bk_recv.at[t, k], grp_peer(k),
            )
            copy.start()
            back[t, k] = copy
        for s in range(slots):
            back_in[group * slots + s, here] = back_out[group * slots + s, here]

        @pl.loop(0, total)
        def _(i):
            spot = down_row(i)
            hidden = jnp.zeros((step, blk), jnp.float32)
            for j in range(total):
                hidden += flag((up_col(j) == spot) & (spot >= 0)) * block_out[j]
            value, _ = gelu_parts(hidden)
            act[i, here] = value.astype(jnp.bfloat16)

    @pl.loop(0, total)
    def _(i):
        term = dot(act[i], y_sel[i], 0, 0) * flag(down_row(i) >= 0)
        dn_out[i] = term.astype(jnp.bfloat16)
        term = dot(x_sel[i], dhid[i], 0, 0) * flag(up_col(i) >= 0)
        up_out[i] = term.astype(jnp.bfloat16)

    grads = []
    for a, (src, dst) in enumerate(((up_out, up_in), (dn_out, dn_in))):
        for k in range(1, rows):
            copy = remote(
                src.at[pl.ds(lax.rem(row + k, rows) * slots, slots)], dst.at[k],
                gr_send.at[a, k], gr_recv.at[a, k], row_peer(k),
            )
            copy.start()
            grads.append(copy)

    def gather_block(spot, here):
        summed = jnp.zeros((step, blk), jnp.float32)
        for j in range(total):
            keep = flag(grp_tab[j // slots, j % slots, 0] == spot)
            summed += keep * back_in[j, here].astype(jnp.float32)
        return summed

    fold = {}
    for t in range(chunks):
        here = pl.ds(t * step, step)
        for k in range(1, rows):
            back[t, k].wait_recv()
        for k in range(1, pairs):

            @pl.loop(0, wide)
            def _(b):
                lanes = pl.ds(pl.multiple_of(b * blk, blk), blk)
                value = gather_block(part_of(k) * wide + b, here)
                fold_out[k, here, lanes] = value.astype(jnp.bfloat16)

            copy = remote(
                fold_out.at[k, here], fold_in.at[k, here],
                fx_send.at[t, k], fx_recv.at[t, k], part_peer(k),
            )
            copy.start()
            fold[t, k] = copy

    for copy in grads:
        copy.wait_recv()
    for src, got, dst in ((up_out, up_in, ugrad_ref), (dn_out, dn_in, dgrad_ref)):
        for s in range(slots):
            summed = src[row * slots + s].astype(jnp.float32)
            for k in range(1, rows):
                summed += got[k, s].astype(jnp.float32)
            dst[s] = summed.astype(jnp.bfloat16)

    for t in range(chunks):
        here = pl.ds(t * step, step)
        for k in range(1, pairs):
            fold[t, k].wait_recv()

        @pl.loop(0, wide)
        def _(b):
            lanes = pl.ds(pl.multiple_of(b * blk, blk), blk)
            value = gather_block(part * wide + b, here)
            for k in range(1, pairs):
                value += fold_in[k, here, lanes].astype(jnp.float32)
            gin_ref[here, lanes] = value.astype(jnp.bfloat16)

    for group_of in (swap, sel, back, fold):
        for copy in group_of.values():
            copy.wait_send()
    for copy in mats + grads:
        copy.wait_send()


def body(rows, cols, inputs, grad_out, up_blocks, up_where, down_blocks, down_where):
    pairs = cols // rows
    slots, blk = up_blocks.shape[:2]
    tok, width = inputs.shape
    total = rows * slots
    chunks = CHUNKS
    bf, f32 = jnp.bfloat16, jnp.float32
    dma = pltpu.SemaphoreType.DMA
    vmem, smem = pltpu.VMEM, pltpu.SMEM
    step = tok // chunks
    scratch = [
        vmem((8, 128), jnp.int32),
        vmem((rows, 8, 128), jnp.int32),
        vmem((rows, 8, 128), jnp.int32),
        smem((rows, 8, 128), jnp.int32),
        smem((rows, 8, 128), jnp.int32),
        [vmem((pairs * width // blk, step, blk), bf) for _ in range(chunks)],
        [vmem((pairs * width // blk, step, blk), bf) for _ in range(chunks)],
        vmem((rows, slots, tok, blk), bf),
        vmem((rows, slots, tok, blk), bf),
        vmem((total, tok, blk), bf),
        vmem((total, tok, blk), bf),
        vmem((total, blk, blk), bf),
        vmem((total, blk, blk), bf),
        vmem((total, step, blk), f32),
        vmem((total, step, blk), f32),
        vmem((total, tok, blk), bf),
        vmem((total, tok, blk), bf),
        vmem((total, tok, blk), bf),
        vmem((total, tok, blk), bf),
        vmem((pairs, tok, width), bf),
        vmem((pairs, tok, width), bf),
        vmem((total, blk, blk), bf),
        vmem((rows, slots, blk, blk), bf),
        vmem((total, blk, blk), bf),
        vmem((rows, slots, blk, blk), bf),
        dma((4,)),
        dma((2, chunks)),
        dma((2,)),
    ]
    for shape in (
        (rows,), (rows,), (2, chunks, pairs), (2, rows),
        (2, chunks, rows), (chunks, rows), (chunks, pairs), (2, rows),
    ):
        scratch += [dma(shape), dma(shape)]
    hbm = pl.BlockSpec(memory_space=pl.ANY)
    small = pl.BlockSpec(memory_space=pltpu.SMEM)
    full = pl.BlockSpec(memory_space=pltpu.VMEM)
    return pl.pallas_call(
        functools.partial(kernel, rows, pairs, slots, chunks),
        out_shape=(
            jax.ShapeDtypeStruct(inputs.shape, bf),
            jax.ShapeDtypeStruct(up_blocks.shape, bf),
            jax.ShapeDtypeStruct(down_blocks.shape, bf),
        ),
        in_specs=[hbm, hbm, hbm, hbm, small, small],
        out_specs=(full, full, full),
        scratch_shapes=scratch,
        compiler_params=pltpu.CompilerParams(collective_id=0, has_side_effects=True),
    )(inputs, grad_out, up_blocks, down_blocks, up_where, down_where)


def solution(mesh):
    rows, cols = mesh.shape["row"], mesh.shape["col"]
    placed = (
        P("row", "col"),
        P("row", "col"),
        P("row", "col", None),
        P("row", "col"),
        P("row", "col", None),
        P("row", "col"),
    )
    return jax.shard_map(
        functools.partial(body, rows, cols),
        mesh=mesh,
        in_specs=placed,
        out_specs=(P("row", "col"), P("row", "col", None), P("row", "col", None)),
        check_vma=False,
    )
```

```python
import functools

import jax
import jax.numpy as jnp
from jax import lax
from jax.experimental import pallas as pl
from jax.experimental.pallas import tpu as pltpu
from jax.sharding import PartitionSpec as P

MESH = pl.DeviceIdType.MESH
CHUNKS = 4


def gelu_parts(hidden):
    cube = hidden * hidden * hidden
    inner = 0.7978845608028654 * (hidden + 0.044715 * cube)
    tanh_val = jnp.tanh(inner)
    value = 0.5 * hidden * (1.0 + tanh_val)
    slope = 0.5 * (1.0 + tanh_val) + 0.5 * hidden * (
        1.0 - tanh_val * tanh_val
    ) * 0.7978845608028654 * (1.0 + 0.134145 * hidden * hidden)
    return (value, slope)


def dot(left, right, left_dim, right_dim):
    return lax.dot_general(
        left, right, (((left_dim,), (right_dim,)), ((), ())),
        preferred_element_type=jnp.float32,
    )


def flag(pred):
    return pred.astype(jnp.float32)


def kernel(
    rows, pairs, slots, chunks,
    x_hbm, y_hbm, up_hbm, dn_hbm, up_hpos, dn_hpos,
    gin_ref, ugrad_ref, dgrad_ref,
    up_pos, dn_pos, own_pos, row_pos, grp_pos, row_tab, grp_tab,
    x_all, y_all, x_out, y_out, x_sel, y_sel,
    up_mat, dn_mat, block_out, down_part, home_sum, dhid,
    back_out, back_in, fold_out, fold_in,
    up_out, up_in, dn_out, dn_in,
    loc_sem, own_sem, tab_sem,
    rp_send, rp_recv, gp_send, gp_recv, ex_send, ex_recv, w_send, w_recv,
    sel_send, sel_recv, bk_send, bk_recv, fx_send, fx_recv, gr_send, gr_recv,
):
    row = lax.axis_index("row")
    col = lax.axis_index("col")
    group, part = col // pairs, col % pairs
    tok = x_hbm.shape[0]
    blk = up_hbm.shape[1]
    wide = x_hbm.shape[1] // blk
    step = tok // chunks
    total = rows * slots

    def row_peer(k):
        return (lax.rem(row + k, rows), col)

    def grp_of(k):
        return lax.rem(group + k, rows)

    def grp_peer(k):
        return (row, grp_of(k) * pairs + part)

    def part_of(k):
        return lax.rem(part + k, pairs)

    def part_peer(k):
        return (row, group * pairs + part_of(k))

    def remote(src, dst, send, recv, peer):
        return pltpu.make_async_remote_copy(
            src_ref=src, dst_ref=dst, send_sem=send, recv_sem=recv,
            device_id=peer, device_id_type=MESH,
        )

    peers = [row_peer(k) for k in range(1, rows)]
    peers += [grp_peer(k) for k in range(1, rows)]
    peers += [part_peer(k) for k in range(1, pairs)]

    barrier = pltpu.get_barrier_semaphore()
    for peer in peers:
        pl.semaphore_signal(barrier, inc=1, device_id=peer, device_id_type=MESH)
    tables = [
        pltpu.make_async_copy(up_hpos, up_pos, tab_sem.at[2]),
        pltpu.make_async_copy(dn_hpos, dn_pos, tab_sem.at[3]),
    ]
    for table in tables:
        table.start()

    mine = pl.ds(row * slots, slots)
    loads = [
        pltpu.make_async_copy(up_hbm, up_mat.at[mine], loc_sem.at[2]),
        pltpu.make_async_copy(dn_hbm, dn_mat.at[mine], loc_sem.at[3]),
    ]
    for load in loads:
        load.start()
    home = pl.ds(part * wide, wide)
    for a, (src, dst) in enumerate(((x_hbm, x_all), (y_hbm, y_all))):
        for t in range(chunks):
            for b in range(wide):
                pltpu.make_async_copy(
                    src.at[pl.ds(t * step, step), pl.ds(b * blk, blk)],
                    dst[t].at[part * wide + b], own_sem.at[a, t],
                ).start()
            loads.append(
                pltpu.make_async_copy(dst[t].at[home], dst[t].at[home], own_sem.at[a, t])
            )
    for table in tables:
        table.wait()
    lane = lax.broadcasted_iota(jnp.int32, (8, 128), 1)
    sub = lax.broadcasted_iota(jnp.int32, (8, 128), 0)
    packed = jnp.full((8, 128), -1, jnp.int32)
    for s in range(slots):
        for j, src in enumerate((up_pos, up_pos, dn_pos, dn_pos)):
            packed = jnp.where((sub == s) & (lane == j), src[s, j % 2], packed)
    own_pos[...] = packed
    row_pos[row] = packed

    pl.semaphore_wait(barrier, len(peers))

    pos_row = []
    for k in range(1, rows):
        copy = remote(own_pos, row_pos.at[row], rp_send.at[k], rp_recv.at[k], row_peer(k))
        copy.start()
        pos_row.append(copy)
    swap = {}
    for t in range(chunks):
        here = pl.ds(t * step, step)
        for a, (src, dst) in enumerate(((x_hbm, x_all), (y_hbm, y_all))):
            for k in range(1, pairs):
                sems = (ex_send.at[a, t, k], ex_recv.at[a, t, k], part_peer(k))
                for b in range(wide):
                    remote(
                        src.at[here, pl.ds(b * blk, blk)],
                        dst[t].at[part * wide + b], *sems,
                    ).start()
                swap[a, t, k] = remote(dst[t].at[home], dst[t].at[home], *sems)
    mats = []
    for a, (src, dst) in enumerate(((up_hbm, up_mat), (dn_hbm, dn_mat))):
        for k in range(1, rows):
            copy = remote(src, dst.at[mine], w_send.at[a, k], w_recv.at[a, k], row_peer(k))
            copy.start()
            mats.append(copy)

    for copy in pos_row:
        copy.wait()
    pos_grp = []
    for k in range(1, rows):
        copy = remote(
            row_pos.at[grp_of(k)], grp_pos.at[group],
            gp_send.at[k], gp_recv.at[k], grp_peer(k),
        )
        copy.start()
        pos_grp.append(copy)
    grp_pos[group] = row_pos[group]
    row_copy = pltpu.make_async_copy(row_pos, row_tab, tab_sem.at[0])
    row_copy.start()
    for copy in pos_grp:
        copy.wait()
    row_copy.wait()
    grp_copy = pltpu.make_async_copy(grp_pos, grp_tab, tab_sem.at[1])
    grp_copy.start()
    grp_copy.wait()
    for load in loads:
        load.wait()

    sel = {}
    for t in range(chunks):
        here = pl.ds(t * step, step)
        for a, (src, out, dst) in enumerate(((x_all, x_out, x_sel), (y_all, y_out, y_sel))):
            for k in range(1, pairs):
                swap[a, t, k].wait_recv()

            def pick(whose, s):
                return src[t][jnp.maximum(grp_tab[whose, s, 3 * a], 0)]

            for k in range(1, rows):
                for s in range(slots):
                    out[k, s, here] = pick(grp_of(k), s)
                copy = remote(
                    out.at[k, :, here], dst.at[pl.ds(group * slots, slots), here],
                    sel_send.at[a, t, k], sel_recv.at[a, t, k], grp_peer(k),
                )
                copy.start()
                sel[a, t, k] = copy
            for s in range(slots):
                dst[group * slots + s, here] = pick(group, s)

    for copy in mats:
        copy.wait_recv()

    def up_col(i):
        return row_tab[i // slots, i % slots, 1]

    def down_row(i):
        return row_tab[i // slots, i % slots, 2]

    def gather_block(spot, t):
        here = pl.ds(t * step, step)
        summed = jnp.zeros((step, blk), jnp.float32)
        for j in range(total):
            keep = flag(grp_tab[j // slots, j % slots, 0] == spot)
            summed += keep * back_in[j, here].astype(jnp.float32)
        return summed

    back, fold = {}, {}

    def send_fold(t):
        here = pl.ds(t * step, step)
        for k in range(1, rows):
            back[t, k].wait_recv()
        for k in range(1, pairs):

            @pl.loop(0, wide)
            def _(b):
                lanes = pl.ds(pl.multiple_of(b * blk, blk), blk)
                value = gather_block(part_of(k) * wide + b, t)
                fold_out[k, here, lanes] = value.astype(jnp.bfloat16)

            copy = remote(
                fold_out.at[k, here], fold_in.at[k, here],
                fx_send.at[t, k], fx_recv.at[t, k], part_peer(k),
            )
            copy.start()
            fold[t, k] = copy

    def sum_home(t):
        @pl.loop(0, wide)
        def _(b):
            lanes = pl.ds(pl.multiple_of(b * blk, blk), blk)
            home_sum[pl.ds(t * step, step), lanes] = gather_block(part * wide + b, t)

    for t in range(chunks):
        here = pl.ds(t * step, step)
        for a in range(2):
            for k in range(1, rows):
                sel[a, t, k].wait_recv()

        @pl.loop(0, total)
        def _(i):
            block_out[i, here] = dot(x_sel[i, here], up_mat[i], 1, 0)
            down_part[i] = dot(y_sel[i, here], dn_mat[i], 1, 1)

        @pl.loop(0, total)
        def _(i):
            spot = up_col(i)
            hidden = jnp.zeros((step, blk), jnp.float32)
            grad = jnp.zeros((step, blk), jnp.float32)
            for j in range(total):
                hidden += flag((up_col(j) == spot) & (spot >= 0)) * block_out[j, here]
                grad += flag((down_row(j) == spot) & (spot >= 0)) * down_part[j]
            _, slope = gelu_parts(hidden)
            dh = (grad * slope).astype(jnp.bfloat16)
            dhid[i, here] = dh
            back_out[i, here] = dot(dh, up_mat[i], 1, 1).astype(jnp.bfloat16)

        for k in range(1, rows):
            copy = remote(
                back_out.at[pl.ds(grp_of(k) * slots, slots), here],
                back_in.at[pl.ds(group * slots, slots), here],
                bk_send.at[t, k], bk_recv.at[t, k], grp_peer(k),
            )
            copy.start()
            back[t, k] = copy
        for s in range(slots):
            back_in[group * slots + s, here] = back_out[group * slots + s, here]
        if t > 0:
            send_fold(t - 1)

    @pl.loop(0, total)
    def _(i):
        spot = down_row(i)
        hidden = jnp.zeros((tok, blk), jnp.float32)
        for j in range(total):
            hidden += flag((up_col(j) == spot) & (spot >= 0)) * block_out[j]
        value, _ = gelu_parts(hidden)
        act = value.astype(jnp.bfloat16)
        term = dot(act, y_sel[i], 0, 0) * flag(spot >= 0)
        dn_out[i] = term.astype(jnp.bfloat16)
        term = dot(x_sel[i], dhid[i], 0, 0) * flag(up_col(i) >= 0)
        up_out[i] = term.astype(jnp.bfloat16)

    grads = []
    for a, (src, dst) in enumerate(((up_out, up_in), (dn_out, dn_in))):
        for k in range(1, rows):
            copy = remote(
                src.at[pl.ds(lax.rem(row + k, rows) * slots, slots)], dst.at[k],
                gr_send.at[a, k], gr_recv.at[a, k], row_peer(k),
            )
            copy.start()
            grads.append(copy)

    send_fold(chunks - 1)
    for t in range(chunks):
        sum_home(t)

    for t in range(chunks):
        here = pl.ds(t * step, step)
        value = home_sum[here]
        for k in range(1, pairs):
            fold[t, k].wait_recv()
            value += fold_in[k, here].astype(jnp.float32)
        gin_ref[here] = value.astype(jnp.bfloat16)

    for copy in grads:
        copy.wait_recv()
    for src, got, dst in ((up_out, up_in, ugrad_ref), (dn_out, dn_in, dgrad_ref)):
        for s in range(slots):
            summed = src[row * slots + s].astype(jnp.float32)
            for k in range(1, rows):
                summed += got[k, s].astype(jnp.float32)
            dst[s] = summed.astype(jnp.bfloat16)

    for group_of in (swap, sel, back, fold):
        for copy in group_of.values():
            copy.wait_send()
    for copy in mats + grads:
        copy.wait_send()


def body(rows, cols, inputs, grad_out, up_blocks, up_where, down_blocks, down_where):
    pairs = cols // rows
    slots, blk = up_blocks.shape[:2]
    tok, width = inputs.shape
    total = rows * slots
    chunks = CHUNKS
    bf, f32 = jnp.bfloat16, jnp.float32
    dma = pltpu.SemaphoreType.DMA
    vmem, smem = pltpu.VMEM, pltpu.SMEM
    step = tok // chunks
    scratch = [
        smem((slots, 2), jnp.int32),
        smem((slots, 2), jnp.int32),
        vmem((8, 128), jnp.int32),
        vmem((rows, 8, 128), jnp.int32),
        vmem((rows, 8, 128), jnp.int32),
        smem((rows, 8, 128), jnp.int32),
        smem((rows, 8, 128), jnp.int32),
        [vmem((pairs * width // blk, step, blk), bf) for _ in range(chunks)],
        [vmem((pairs * width // blk, step, blk), bf) for _ in range(chunks)],
        vmem((rows, slots, tok, blk), bf),
        vmem((rows, slots, tok, blk), bf),
        vmem((total, tok, blk), bf),
        vmem((total, tok, blk), bf),
        vmem((total, blk, blk), bf),
        vmem((total, blk, blk), bf),
        vmem((total, tok, blk), f32),
        vmem((total, step, blk), f32),
        vmem((tok, width), f32),
        vmem((total, tok, blk), bf),
        vmem((total, tok, blk), bf),
        vmem((total, tok, blk), bf),
        vmem((pairs, tok, width), bf),
        vmem((pairs, tok, width), bf),
        vmem((total, blk, blk), bf),
        vmem((rows, slots, blk, blk), bf),
        vmem((total, blk, blk), bf),
        vmem((rows, slots, blk, blk), bf),
        dma((4,)),
        dma((2, chunks)),
        dma((4,)),
    ]
    for shape in (
        (rows,), (rows,), (2, chunks, pairs), (2, rows),
        (2, chunks, rows), (chunks, rows), (chunks, pairs), (2, rows),
    ):
        scratch += [dma(shape), dma(shape)]
    hbm = pl.BlockSpec(memory_space=pl.ANY)
    full = pl.BlockSpec(memory_space=pltpu.VMEM)
    return pl.pallas_call(
        functools.partial(kernel, rows, pairs, slots, chunks),
        out_shape=(
            jax.ShapeDtypeStruct(inputs.shape, bf),
            jax.ShapeDtypeStruct(up_blocks.shape, bf),
            jax.ShapeDtypeStruct(down_blocks.shape, bf),
        ),
        in_specs=[hbm] * 6,
        out_specs=(full, full, full),
        scratch_shapes=scratch,
        compiler_params=pltpu.CompilerParams(collective_id=0, has_side_effects=True),
    )(inputs, grad_out, up_blocks, down_blocks, up_where, down_where)


def solution(mesh):
    rows, cols = mesh.shape["row"], mesh.shape["col"]
    placed = (
        P("row", "col"),
        P("row", "col"),
        P("row", "col", None),
        P("row", "col"),
        P("row", "col", None),
        P("row", "col"),
    )
    return jax.shard_map(
        functools.partial(body, rows, cols),
        mesh=mesh,
        in_specs=placed,
        out_specs=(P("row", "col"), P("row", "col", None), P("row", "col", None)),
        check_vma=False,
    )
```

```python
import functools

import jax
import jax.numpy as jnp
from jax import lax
from jax.experimental import pallas as pl
from jax.experimental.pallas import tpu as pltpu
from jax.sharding import PartitionSpec as P

MESH = pl.DeviceIdType.MESH
CHUNKS = 2


def gelu_parts(hidden):
    cube = hidden * hidden * hidden
    inner = 0.7978845608028654 * (hidden + 0.044715 * cube)
    tanh_val = jnp.tanh(inner)
    value = 0.5 * hidden * (1.0 + tanh_val)
    slope = 0.5 * (1.0 + tanh_val) + 0.5 * hidden * (
        1.0 - tanh_val * tanh_val
    ) * 0.7978845608028654 * (1.0 + 0.134145 * hidden * hidden)
    return (value, slope)


def dot(left, right, left_dim, right_dim):
    return lax.dot_general(
        left, right, (((left_dim,), (right_dim,)), ((), ())),
        preferred_element_type=jnp.float32,
    )


def flag(pred):
    return pred.astype(jnp.float32)


def kernel(
    rows, pairs, slots, chunks,
    x_hbm, y_hbm, up_hbm, dn_hbm, up_hpos, dn_hpos,
    gin_ref, ugrad_ref, dgrad_ref,
    up_pos, dn_pos, own_pos, row_pos, grp_pos, row_tab, grp_tab,
    x_all, y_all, x_out, y_out, x_sel, y_sel,
    up_mat, dn_mat, block_out, down_part, home_sum, dhid,
    back_out, back_in, fold_out, fold_in,
    up_out, up_in, dn_out, dn_in,
    loc_sem, own_sem, tab_sem,
    rp_send, rp_recv, gp_send, gp_recv, ex_send, ex_recv, w_send, w_recv,
    sel_send, sel_recv, bk_send, bk_recv, fx_send, fx_recv, gr_send, gr_recv,
):
    row = lax.axis_index("row")
    col = lax.axis_index("col")
    group, part = col // pairs, col % pairs
    tok = x_hbm.shape[0]
    blk = up_hbm.shape[1]
    wide = x_hbm.shape[1] // blk
    step = tok // chunks
    total = rows * slots

    def row_peer(k):
        return (lax.rem(row + k, rows), col)

    def grp_of(k):
        return lax.rem(group + k, rows)

    def grp_peer(k):
        return (row, grp_of(k) * pairs + part)

    def part_of(k):
        return lax.rem(part + k, pairs)

    def part_peer(k):
        return (row, group * pairs + part_of(k))

    def remote(src, dst, send, recv, peer):
        return pltpu.make_async_remote_copy(
            src_ref=src, dst_ref=dst, send_sem=send, recv_sem=recv,
            device_id=peer, device_id_type=MESH,
        )

    peers = [row_peer(k) for k in range(1, rows)]
    peers += [grp_peer(k) for k in range(1, rows)]
    peers += [part_peer(k) for k in range(1, pairs)]

    barrier = pltpu.get_barrier_semaphore()
    for peer in peers:
        pl.semaphore_signal(barrier, inc=1, device_id=peer, device_id_type=MESH)
    tables = [
        pltpu.make_async_copy(up_hpos, up_pos, tab_sem.at[2]),
        pltpu.make_async_copy(dn_hpos, dn_pos, tab_sem.at[3]),
    ]
    for table in tables:
        table.start()

    mine = pl.ds(row * slots, slots)
    loads = [
        pltpu.make_async_copy(up_hbm, up_mat.at[mine], loc_sem.at[2]),
        pltpu.make_async_copy(dn_hbm, dn_mat.at[mine], loc_sem.at[3]),
    ]
    for load in loads:
        load.start()
    home = pl.ds(part * wide, wide)
    for a, (src, dst) in enumerate(((x_hbm, x_all), (y_hbm, y_all))):
        for t in range(chunks):
            for b in range(wide):
                pltpu.make_async_copy(
                    src.at[pl.ds(t * step, step), pl.ds(b * blk, blk)],
                    dst[t].at[part * wide + b], own_sem.at[a, t],
                ).start()
            loads.append(
                pltpu.make_async_copy(dst[t].at[home], dst[t].at[home], own_sem.at[a, t])
            )
    for table in tables:
        table.wait()
    lane = lax.broadcasted_iota(jnp.int32, (8, 128), 1)
    sub = lax.broadcasted_iota(jnp.int32, (8, 128), 0)
    packed = jnp.full((8, 128), -1, jnp.int32)
    for s in range(slots):
        for j, src in enumerate((up_pos, up_pos, dn_pos, dn_pos)):
            packed = jnp.where((sub == s) & (lane == j), src[s, j % 2], packed)
    own_pos[...] = packed
    row_pos[row] = packed

    pl.semaphore_wait(barrier, len(peers))

    pos_row = []
    for k in range(1, rows):
        copy = remote(own_pos, row_pos.at[row], rp_send.at[k], rp_recv.at[k], row_peer(k))
        copy.start()
        pos_row.append(copy)
    swap = {}
    for t in range(chunks):
        here = pl.ds(t * step, step)
        for a, (src, dst) in enumerate(((x_hbm, x_all), (y_hbm, y_all))):
            for k in range(1, pairs):
                sems = (ex_send.at[a, t, k], ex_recv.at[a, t, k], part_peer(k))
                for b in range(wide):
                    remote(
                        src.at[here, pl.ds(b * blk, blk)],
                        dst[t].at[part * wide + b], *sems,
                    ).start()
                swap[a, t, k] = remote(dst[t].at[home], dst[t].at[home], *sems)
    mats = []
    for a, (src, dst) in enumerate(((up_hbm, up_mat), (dn_hbm, dn_mat))):
        for k in range(1, rows):
            copy = remote(src, dst.at[mine], w_send.at[a, k], w_recv.at[a, k], row_peer(k))
            copy.start()
            mats.append(copy)

    for copy in pos_row:
        copy.wait()
    pos_grp = []
    for k in range(1, rows):
        copy = remote(
            row_pos.at[grp_of(k)], grp_pos.at[group],
            gp_send.at[k], gp_recv.at[k], grp_peer(k),
        )
        copy.start()
        pos_grp.append(copy)
    grp_pos[group] = row_pos[group]
    row_copy = pltpu.make_async_copy(row_pos, row_tab, tab_sem.at[0])
    row_copy.start()
    for copy in pos_grp:
        copy.wait()
    row_copy.wait()
    grp_copy = pltpu.make_async_copy(grp_pos, grp_tab, tab_sem.at[1])
    grp_copy.start()
    grp_copy.wait()
    for load in loads:
        load.wait()

    sel = {}
    for t in range(chunks):
        here = pl.ds(t * step, step)
        for a, (src, out, dst) in enumerate(((x_all, x_out, x_sel), (y_all, y_out, y_sel))):
            for k in range(1, pairs):
                swap[a, t, k].wait_recv()

            def pick(whose, s):
                return src[t][jnp.maximum(grp_tab[whose, s, 3 * a], 0)]

            for k in range(1, rows):
                for s in range(slots):
                    out[k, s, here] = pick(grp_of(k), s)
                copy = remote(
                    out.at[k, :, here], dst.at[pl.ds(group * slots, slots), here],
                    sel_send.at[a, t, k], sel_recv.at[a, t, k], grp_peer(k),
                )
                copy.start()
                sel[a, t, k] = copy
            for s in range(slots):
                dst[group * slots + s, here] = pick(group, s)

    for copy in mats:
        copy.wait_recv()

    def up_col(i):
        return row_tab[i // slots, i % slots, 1]

    def down_row(i):
        return row_tab[i // slots, i % slots, 2]

    def gather_block(spot, t):
        here = pl.ds(t * step, step)
        summed = jnp.zeros((step, blk), jnp.float32)
        for j in range(total):
            keep = flag(grp_tab[j // slots, j % slots, 0] == spot)
            summed += keep * back_in[j, here].astype(jnp.float32)
        return summed

    back, fold = {}, {}

    def send_fold(t):
        here = pl.ds(t * step, step)
        for k in range(1, rows):
            back[t, k].wait_recv()
        for k in range(1, pairs):

            @pl.loop(0, wide)
            def _(b):
                lanes = pl.ds(pl.multiple_of(b * blk, blk), blk)
                value = gather_block(part_of(k) * wide + b, t)
                fold_out[k, here, lanes] = value.astype(jnp.bfloat16)

            copy = remote(
                fold_out.at[k, here], fold_in.at[k, here],
                fx_send.at[t, k], fx_recv.at[t, k], part_peer(k),
            )
            copy.start()
            fold[t, k] = copy

    def sum_home(t):
        @pl.loop(0, wide)
        def _(b):
            lanes = pl.ds(pl.multiple_of(b * blk, blk), blk)
            home_sum[pl.ds(t * step, step), lanes] = gather_block(part * wide + b, t)

    for t in range(chunks):
        here = pl.ds(t * step, step)
        for a in range(2):
            for k in range(1, rows):
                sel[a, t, k].wait_recv()

        @pl.loop(0, total)
        def _(i):
            block_out[i, here] = dot(x_sel[i, here], up_mat[i], 1, 0)
            down_part[i] = dot(y_sel[i, here], dn_mat[i], 1, 1)

        @pl.loop(0, total)
        def _(i):
            spot = up_col(i)
            hidden = jnp.zeros((step, blk), jnp.float32)
            grad = jnp.zeros((step, blk), jnp.float32)
            for j in range(total):
                hidden += flag((up_col(j) == spot) & (spot >= 0)) * block_out[j, here]
                grad += flag((down_row(j) == spot) & (spot >= 0)) * down_part[j]
            _, slope = gelu_parts(hidden)
            dh = (grad * slope).astype(jnp.bfloat16)
            dhid[i, here] = dh
            back_out[i, here] = dot(dh, up_mat[i], 1, 1).astype(jnp.bfloat16)

        for k in range(1, rows):
            copy = remote(
                back_out.at[pl.ds(grp_of(k) * slots, slots), here],
                back_in.at[pl.ds(group * slots, slots), here],
                bk_send.at[t, k], bk_recv.at[t, k], grp_peer(k),
            )
            copy.start()
            back[t, k] = copy
        for s in range(slots):
            back_in[group * slots + s, here] = back_out[group * slots + s, here]
        if t > 0:
            send_fold(t - 1)

    @pl.loop(0, total)
    def _(i):
        spot = down_row(i)
        hidden = jnp.zeros((tok, blk), jnp.float32)
        for j in range(total):
            hidden += flag((up_col(j) == spot) & (spot >= 0)) * block_out[j]
        value, _ = gelu_parts(hidden)
        act = value.astype(jnp.bfloat16)
        term = dot(act, y_sel[i], 0, 0) * flag(spot >= 0)
        dn_out[i] = term.astype(jnp.bfloat16)
        term = dot(x_sel[i], dhid[i], 0, 0) * flag(up_col(i) >= 0)
        up_out[i] = term.astype(jnp.bfloat16)

    grads = []
    for a, (src, dst) in enumerate(((up_out, up_in), (dn_out, dn_in))):
        for k in range(1, rows):
            copy = remote(
                src.at[pl.ds(lax.rem(row + k, rows) * slots, slots)], dst.at[k],
                gr_send.at[a, k], gr_recv.at[a, k], row_peer(k),
            )
            copy.start()
            grads.append(copy)

    send_fold(chunks - 1)
    for t in range(chunks):
        sum_home(t)

    for t in range(chunks):
        here = pl.ds(t * step, step)
        value = home_sum[here]
        for k in range(1, pairs):
            fold[t, k].wait_recv()
            value += fold_in[k, here].astype(jnp.float32)
        gin_ref[here] = value.astype(jnp.bfloat16)

    for copy in grads:
        copy.wait_recv()
    for src, got, dst in ((up_out, up_in, ugrad_ref), (dn_out, dn_in, dgrad_ref)):
        for s in range(slots):
            summed = src[row * slots + s].astype(jnp.float32)
            for k in range(1, rows):
                summed += got[k, s].astype(jnp.float32)
            dst[s] = summed.astype(jnp.bfloat16)

    for group_of in (swap, sel, back, fold):
        for copy in group_of.values():
            copy.wait_send()
    for copy in mats + grads:
        copy.wait_send()


def body(rows, cols, inputs, grad_out, up_blocks, up_where, down_blocks, down_where):
    pairs = cols // rows
    slots, blk = up_blocks.shape[:2]
    tok, width = inputs.shape
    total = rows * slots
    chunks = CHUNKS
    bf, f32 = jnp.bfloat16, jnp.float32
    dma = pltpu.SemaphoreType.DMA
    vmem, smem = pltpu.VMEM, pltpu.SMEM
    step = tok // chunks
    scratch = [
        smem((slots, 2), jnp.int32),
        smem((slots, 2), jnp.int32),
        vmem((8, 128), jnp.int32),
        vmem((rows, 8, 128), jnp.int32),
        vmem((rows, 8, 128), jnp.int32),
        smem((rows, 8, 128), jnp.int32),
        smem((rows, 8, 128), jnp.int32),
        [vmem((pairs * width // blk, step, blk), bf) for _ in range(chunks)],
        [vmem((pairs * width // blk, step, blk), bf) for _ in range(chunks)],
        vmem((rows, slots, tok, blk), bf),
        vmem((rows, slots, tok, blk), bf),
        vmem((total, tok, blk), bf),
        vmem((total, tok, blk), bf),
        vmem((total, blk, blk), bf),
        vmem((total, blk, blk), bf),
        vmem((total, tok, blk), f32),
        vmem((total, step, blk), f32),
        vmem((tok, width), f32),
        vmem((total, tok, blk), bf),
        vmem((total, tok, blk), bf),
        vmem((total, tok, blk), bf),
        vmem((pairs, tok, width), bf),
        vmem((pairs, tok, width), bf),
        vmem((total, blk, blk), bf),
        vmem((rows, slots, blk, blk), bf),
        vmem((total, blk, blk), bf),
        vmem((rows, slots, blk, blk), bf),
        dma((4,)),
        dma((2, chunks)),
        dma((4,)),
    ]
    for shape in (
        (rows,), (rows,), (2, chunks, pairs), (2, rows),
        (2, chunks, rows), (chunks, rows), (chunks, pairs), (2, rows),
    ):
        scratch += [dma(shape), dma(shape)]
    hbm = pl.BlockSpec(memory_space=pl.ANY)
    full = pl.BlockSpec(memory_space=pltpu.VMEM)
    return pl.pallas_call(
        functools.partial(kernel, rows, pairs, slots, chunks),
        out_shape=(
            jax.ShapeDtypeStruct(inputs.shape, bf),
            jax.ShapeDtypeStruct(up_blocks.shape, bf),
            jax.ShapeDtypeStruct(down_blocks.shape, bf),
        ),
        in_specs=[hbm] * 6,
        out_specs=(full, full, full),
        scratch_shapes=scratch,
        compiler_params=pltpu.CompilerParams(collective_id=0, has_side_effects=True),
    )(inputs, grad_out, up_blocks, down_blocks, up_where, down_where)


def solution(mesh):
    rows, cols = mesh.shape["row"], mesh.shape["col"]
    placed = (
        P("row", "col"),
        P("row", "col"),
        P("row", "col", None),
        P("row", "col"),
        P("row", "col", None),
        P("row", "col"),
    )
    return jax.shard_map(
        functools.partial(body, rows, cols),
        mesh=mesh,
        in_specs=placed,
        out_specs=(P("row", "col"), P("row", "col", None), P("row", "col", None)),
        check_vma=False,
    )
```

```python
import functools

import jax
import jax.numpy as jnp
from jax import lax
from jax.experimental import pallas as pl
from jax.experimental.pallas import tpu as pltpu
from jax.sharding import PartitionSpec as P

MESH = pl.DeviceIdType.MESH
CHUNKS = 2


def gelu_parts(hidden):
    cube = hidden * hidden * hidden
    inner = 0.7978845608028654 * (hidden + 0.044715 * cube)
    tanh_val = jnp.tanh(inner)
    value = 0.5 * hidden * (1.0 + tanh_val)
    slope = 0.5 * (1.0 + tanh_val) + 0.5 * hidden * (
        1.0 - tanh_val * tanh_val
    ) * 0.7978845608028654 * (1.0 + 0.134145 * hidden * hidden)
    return (value, slope)


def dot(left, right, left_dim, right_dim):
    return lax.dot_general(
        left, right, (((left_dim,), (right_dim,)), ((), ())),
        preferred_element_type=jnp.float32,
    )


def each(count, unroll=8):
    size = max(n for n in range(1, unroll + 1) if count % n == 0)

    def run(body):
        if size == count:
            for i in range(count):
                body(i)
            return

        @pl.loop(0, count // size)
        def _(outer):
            for i in range(size):
                body(outer * size + i)

    return run


def flag(pred):
    return pred.astype(jnp.float32)


def kernel(
    rows, pairs, slots, chunks,
    x_hbm, y_hbm, up_hbm, dn_hbm, up_hpos, dn_hpos,
    gin_ref, ugrad_ref, dgrad_ref,
    up_pos, dn_pos, own_pos, row_pos, grp_pos, row_tab, grp_tab,
    x_all, y_all, x_out, y_out, x_sel, y_sel,
    up_mat, dn_mat, block_out, down_part, home_sum, dhid,
    back_out, back_in, fold_out, fold_in,
    up_out, up_in, dn_out, dn_in,
    loc_sem, own_sem, tab_sem,
    rp_send, rp_recv, gp_send, gp_recv, ex_send, ex_recv, w_send, w_recv,
    sel_send, sel_recv, bk_send, bk_recv, fx_send, fx_recv, gr_send, gr_recv,
):
    row = lax.axis_index("row")
    col = lax.axis_index("col")
    group, part = col // pairs, col % pairs
    tok = x_hbm.shape[0]
    blk = up_hbm.shape[1]
    wide = x_hbm.shape[1] // blk
    step = tok // chunks
    total = rows * slots

    def row_peer(k):
        return (lax.rem(row + k, rows), col)

    def grp_of(k):
        return lax.rem(group + k, rows)

    def grp_peer(k):
        return (row, grp_of(k) * pairs + part)

    def part_of(k):
        return lax.rem(part + k, pairs)

    def part_peer(k):
        return (row, group * pairs + part_of(k))

    def remote(src, dst, send, recv, peer):
        return pltpu.make_async_remote_copy(
            src_ref=src, dst_ref=dst, send_sem=send, recv_sem=recv,
            device_id=peer, device_id_type=MESH,
        )

    peers = [row_peer(k) for k in range(1, rows)]
    peers += [grp_peer(k) for k in range(1, rows)]
    peers += [part_peer(k) for k in range(1, pairs)]

    barrier = pltpu.get_barrier_semaphore()
    for peer in peers:
        pl.semaphore_signal(barrier, inc=1, device_id=peer, device_id_type=MESH)
    tables = [
        pltpu.make_async_copy(up_hpos, up_pos, tab_sem.at[2]),
        pltpu.make_async_copy(dn_hpos, dn_pos, tab_sem.at[3]),
    ]
    for table in tables:
        table.start()

    mine = pl.ds(row * slots, slots)
    loads = [
        pltpu.make_async_copy(up_hbm, up_mat.at[mine], loc_sem.at[2]),
        pltpu.make_async_copy(dn_hbm, dn_mat.at[mine], loc_sem.at[3]),
    ]
    for load in loads:
        load.start()
    home = pl.ds(part * wide, wide)
    for a, (src, dst) in enumerate(((x_hbm, x_all), (y_hbm, y_all))):
        for t in range(chunks):
            for b in range(wide):
                pltpu.make_async_copy(
                    src.at[pl.ds(t * step, step), pl.ds(b * blk, blk)],
                    dst[t].at[part * wide + b], own_sem.at[a, t],
                ).start()
            loads.append(
                pltpu.make_async_copy(dst[t].at[home], dst[t].at[home], own_sem.at[a, t])
            )
    for table in tables:
        table.wait()
    lane = lax.broadcasted_iota(jnp.int32, (8, 128), 1)
    sub = lax.broadcasted_iota(jnp.int32, (8, 128), 0)
    packed = jnp.full((8, 128), -1, jnp.int32)
    for s in range(slots):
        for j, src in enumerate((up_pos, up_pos, dn_pos, dn_pos)):
            packed = jnp.where((sub == s) & (lane == j), src[s, j % 2], packed)
    own_pos[...] = packed
    row_pos[row] = packed

    pl.semaphore_wait(barrier, len(peers))

    pos_row = []
    for k in range(1, rows):
        copy = remote(own_pos, row_pos.at[row], rp_send.at[k], rp_recv.at[k], row_peer(k))
        copy.start()
        pos_row.append(copy)
    swap = {}
    for t in range(chunks):
        here = pl.ds(t * step, step)
        for a, (src, dst) in enumerate(((x_hbm, x_all), (y_hbm, y_all))):
            for k in range(1, pairs):
                sems = (ex_send.at[a, t, k], ex_recv.at[a, t, k], part_peer(k))
                for b in range(wide):
                    remote(
                        src.at[here, pl.ds(b * blk, blk)],
                        dst[t].at[part * wide + b], *sems,
                    ).start()
                swap[a, t, k] = remote(dst[t].at[home], dst[t].at[home], *sems)
    mats = []
    for a, (src, dst) in enumerate(((up_hbm, up_mat), (dn_hbm, dn_mat))):
        for k in range(1, rows):
            copy = remote(src, dst.at[mine], w_send.at[a, k], w_recv.at[a, k], row_peer(k))
            copy.start()
            mats.append(copy)

    for copy in pos_row:
        copy.wait()
    pos_grp = []
    for k in range(1, rows):
        copy = remote(
            row_pos.at[grp_of(k)], grp_pos.at[group],
            gp_send.at[k], gp_recv.at[k], grp_peer(k),
        )
        copy.start()
        pos_grp.append(copy)
    grp_pos[group] = row_pos[group]
    row_copy = pltpu.make_async_copy(row_pos, row_tab, tab_sem.at[0])
    row_copy.start()
    for copy in pos_grp:
        copy.wait()
    row_copy.wait()
    grp_copy = pltpu.make_async_copy(grp_pos, grp_tab, tab_sem.at[1])
    grp_copy.start()
    grp_copy.wait()
    for load in loads:
        load.wait()

    sel = {}
    for t in range(chunks):
        here = pl.ds(t * step, step)
        for a, (src, out, dst) in enumerate(((x_all, x_out, x_sel), (y_all, y_out, y_sel))):
            for k in range(1, pairs):
                swap[a, t, k].wait_recv()

            def pick(whose, s):
                return src[t][jnp.maximum(grp_tab[whose, s, 3 * a], 0)]

            for k in range(1, rows):
                for s in range(slots):
                    out[k, s, here] = pick(grp_of(k), s)
                copy = remote(
                    out.at[k, :, here], dst.at[pl.ds(group * slots, slots), here],
                    sel_send.at[a, t, k], sel_recv.at[a, t, k], grp_peer(k),
                )
                copy.start()
                sel[a, t, k] = copy
            for s in range(slots):
                dst[group * slots + s, here] = pick(group, s)

    for copy in mats:
        copy.wait_recv()

    def up_col(i):
        return row_tab[i // slots, i % slots, 1]

    def down_row(i):
        return row_tab[i // slots, i % slots, 2]

    def gather_block(spot, t):
        here = pl.ds(t * step, step)
        summed = jnp.zeros((step, blk), jnp.float32)
        for j in range(total):
            keep = flag(grp_tab[j // slots, j % slots, 0] == spot)
            summed += keep * back_in[j, here].astype(jnp.float32)
        return summed

    back, fold = {}, {}

    def send_fold(t):
        here = pl.ds(t * step, step)
        for k in range(1, rows):
            back[t, k].wait_recv()
        for k in range(1, pairs):

            @pl.loop(0, wide)
            def _(b):
                lanes = pl.ds(pl.multiple_of(b * blk, blk), blk)
                value = gather_block(part_of(k) * wide + b, t)
                fold_out[k, here, lanes] = value.astype(jnp.bfloat16)

            copy = remote(
                fold_out.at[k, here], fold_in.at[k, here],
                fx_send.at[t, k], fx_recv.at[t, k], part_peer(k),
            )
            copy.start()
            fold[t, k] = copy

    def sum_home(t):
        @pl.loop(0, wide)
        def _(b):
            lanes = pl.ds(pl.multiple_of(b * blk, blk), blk)
            home_sum[pl.ds(t * step, step), lanes] = gather_block(part * wide + b, t)

    for t in range(chunks):
        here = pl.ds(t * step, step)
        for a in range(2):
            for k in range(1, rows):
                sel[a, t, k].wait_recv()

        @each(total)
        def _(i):
            block_out[i, here] = dot(x_sel[i, here], up_mat[i], 1, 0)
            down_part[i] = dot(y_sel[i, here], dn_mat[i], 1, 1)

        @each(total)
        def _(i):
            spot = up_col(i)
            hidden = jnp.zeros((step, blk), jnp.float32)
            grad = jnp.zeros((step, blk), jnp.float32)
            for j in range(total):
                hidden += flag((up_col(j) == spot) & (spot >= 0)) * block_out[j, here]
                grad += flag((down_row(j) == spot) & (spot >= 0)) * down_part[j]
            _, slope = gelu_parts(hidden)
            dh = (grad * slope).astype(jnp.bfloat16)
            dhid[i, here] = dh
            back_out[i, here] = dot(dh, up_mat[i], 1, 1).astype(jnp.bfloat16)

        for k in range(1, rows):
            copy = remote(
                back_out.at[pl.ds(grp_of(k) * slots, slots), here],
                back_in.at[pl.ds(group * slots, slots), here],
                bk_send.at[t, k], bk_recv.at[t, k], grp_peer(k),
            )
            copy.start()
            back[t, k] = copy
        for s in range(slots):
            back_in[group * slots + s, here] = back_out[group * slots + s, here]
        if t > 0:
            send_fold(t - 1)

    @each(total)
    def _(i):
        spot = down_row(i)
        hidden = jnp.zeros((tok, blk), jnp.float32)
        for j in range(total):
            hidden += flag((up_col(j) == spot) & (spot >= 0)) * block_out[j]
        value, _ = gelu_parts(hidden)
        act = value.astype(jnp.bfloat16)
        term = dot(act, y_sel[i], 0, 0) * flag(spot >= 0)
        dn_out[i] = term.astype(jnp.bfloat16)
        term = dot(x_sel[i], dhid[i], 0, 0) * flag(up_col(i) >= 0)
        up_out[i] = term.astype(jnp.bfloat16)

    grads = []
    for a, (src, dst) in enumerate(((up_out, up_in), (dn_out, dn_in))):
        for k in range(1, rows):
            copy = remote(
                src.at[pl.ds(lax.rem(row + k, rows) * slots, slots)], dst.at[k],
                gr_send.at[a, k], gr_recv.at[a, k], row_peer(k),
            )
            copy.start()
            grads.append(copy)

    send_fold(chunks - 1)
    for t in range(chunks):
        sum_home(t)

    for t in range(chunks):
        here = pl.ds(t * step, step)
        value = home_sum[here]
        for k in range(1, pairs):
            fold[t, k].wait_recv()
            value += fold_in[k, here].astype(jnp.float32)
        gin_ref[here] = value.astype(jnp.bfloat16)

    for copy in grads:
        copy.wait_recv()
    for src, got, dst in ((up_out, up_in, ugrad_ref), (dn_out, dn_in, dgrad_ref)):
        for s in range(slots):
            summed = src[row * slots + s].astype(jnp.float32)
            for k in range(1, rows):
                summed += got[k, s].astype(jnp.float32)
            dst[s] = summed.astype(jnp.bfloat16)

    for group_of in (swap, sel, back, fold):
        for copy in group_of.values():
            copy.wait_send()
    for copy in mats + grads:
        copy.wait_send()


def body(rows, cols, inputs, grad_out, up_blocks, up_where, down_blocks, down_where):
    pairs = cols // rows
    slots, blk = up_blocks.shape[:2]
    tok, width = inputs.shape
    total = rows * slots
    chunks = CHUNKS
    bf, f32 = jnp.bfloat16, jnp.float32
    dma = pltpu.SemaphoreType.DMA
    vmem, smem = pltpu.VMEM, pltpu.SMEM
    step = tok // chunks
    scratch = [
        smem((slots, 2), jnp.int32),
        smem((slots, 2), jnp.int32),
        vmem((8, 128), jnp.int32),
        vmem((rows, 8, 128), jnp.int32),
        vmem((rows, 8, 128), jnp.int32),
        smem((rows, 8, 128), jnp.int32),
        smem((rows, 8, 128), jnp.int32),
        [vmem((pairs * width // blk, step, blk), bf) for _ in range(chunks)],
        [vmem((pairs * width // blk, step, blk), bf) for _ in range(chunks)],
        vmem((rows, slots, tok, blk), bf),
        vmem((rows, slots, tok, blk), bf),
        vmem((total, tok, blk), bf),
        vmem((total, tok, blk), bf),
        vmem((total, blk, blk), bf),
        vmem((total, blk, blk), bf),
        vmem((total, tok, blk), f32),
        vmem((total, step, blk), f32),
        vmem((tok, width), f32),
        vmem((total, tok, blk), bf),
        vmem((total, tok, blk), bf),
        vmem((total, tok, blk), bf),
        vmem((pairs, tok, width), bf),
        vmem((pairs, tok, width), bf),
        vmem((total, blk, blk), bf),
        vmem((rows, slots, blk, blk), bf),
        vmem((total, blk, blk), bf),
        vmem((rows, slots, blk, blk), bf),
        dma((4,)),
        dma((2, chunks)),
        dma((4,)),
    ]
    for shape in (
        (rows,), (rows,), (2, chunks, pairs), (2, rows),
        (2, chunks, rows), (chunks, rows), (chunks, pairs), (2, rows),
    ):
        scratch += [dma(shape), dma(shape)]
    hbm = pl.BlockSpec(memory_space=pl.ANY)
    full = pl.BlockSpec(memory_space=pltpu.VMEM)
    return pl.pallas_call(
        functools.partial(kernel, rows, pairs, slots, chunks),
        out_shape=(
            jax.ShapeDtypeStruct(inputs.shape, bf),
            jax.ShapeDtypeStruct(up_blocks.shape, bf),
            jax.ShapeDtypeStruct(down_blocks.shape, bf),
        ),
        in_specs=[hbm] * 6,
        out_specs=(full, full, full),
        scratch_shapes=scratch,
        compiler_params=pltpu.CompilerParams(collective_id=0, has_side_effects=True),
    )(inputs, grad_out, up_blocks, down_blocks, up_where, down_where)


def solution(mesh):
    rows, cols = mesh.shape["row"], mesh.shape["col"]
    placed = (
        P("row", "col"),
        P("row", "col"),
        P("row", "col", None),
        P("row", "col"),
        P("row", "col", None),
        P("row", "col"),
    )
    return jax.shard_map(
        functools.partial(body, rows, cols),
        mesh=mesh,
        in_specs=placed,
        out_specs=(P("row", "col"), P("row", "col", None), P("row", "col", None)),
        check_vma=False,
    )
```

```python
import functools

import jax
import jax.numpy as jnp
from jax import lax
from jax.experimental import pallas as pl
from jax.experimental.pallas import tpu as pltpu
from jax.sharding import PartitionSpec as P

MESH = pl.DeviceIdType.MESH
CHUNKS = 2


def gelu_parts(hidden):
    cube = hidden * hidden * hidden
    inner = 0.7978845608028654 * (hidden + 0.044715 * cube)
    tanh_val = jnp.tanh(inner)
    value = 0.5 * hidden * (1.0 + tanh_val)
    slope = 0.5 * (1.0 + tanh_val) + 0.5 * hidden * (
        1.0 - tanh_val * tanh_val
    ) * 0.7978845608028654 * (1.0 + 0.134145 * hidden * hidden)
    return (value, slope)


def dot(left, right, left_dim, right_dim):
    return lax.dot_general(
        left, right, (((left_dim,), (right_dim,)), ((), ())),
        preferred_element_type=jnp.float32,
    )


def each(count, unroll=8):
    size = max(n for n in range(1, unroll + 1) if count % n == 0)

    def run(body):
        if size == count:
            for i in range(count):
                body(i)
            return

        @pl.loop(0, count // size)
        def _(outer):
            for i in range(size):
                body(outer * size + i)

    return run


def flag(pred):
    return pred.astype(jnp.float32)


def kernel(
    rows, pairs, slots, chunks,
    x_hbm, y_hbm, up_hbm, dn_hbm, up_hpos, dn_hpos,
    gin_ref, ugrad_ref, dgrad_ref,
    up_pos, dn_pos, own_pos, row_pos, grp_pos, row_tab, grp_tab,
    x_all, y_all, x_out, y_out, x_sel, y_sel,
    up_mat, dn_mat, block_out, down_part, home_sum, dhid,
    back_out, back_in, fold_out, fold_in,
    up_out, up_in, dn_out, dn_in,
    loc_sem, own_sem, tab_sem,
    rp_send, rp_recv, gp_send, gp_recv, ex_send, ex_recv, w_send, w_recv,
    sel_send, sel_recv, bk_send, bk_recv, fx_send, fx_recv, gr_send, gr_recv,
):
    row = lax.axis_index("row")
    col = lax.axis_index("col")
    group, part = col // pairs, col % pairs
    tok = x_hbm.shape[0]
    blk = up_hbm.shape[1]
    wide = x_hbm.shape[1] // blk
    step = tok // chunks
    total = rows * slots

    def row_peer(k):
        return (lax.rem(row + k, rows), col)

    def grp_of(k):
        return lax.rem(group + k, rows)

    def grp_peer(k):
        return (row, grp_of(k) * pairs + part)

    def part_of(k):
        return lax.rem(part + k, pairs)

    def part_peer(k):
        return (row, group * pairs + part_of(k))

    def remote(src, dst, send, recv, peer):
        return pltpu.make_async_remote_copy(
            src_ref=src, dst_ref=dst, send_sem=send, recv_sem=recv,
            device_id=peer, device_id_type=MESH,
        )

    def pick_peer(k):
        return (lax.rem(row + k, rows), row * pairs + part)

    def pick_source(k):
        return (group, grp_of(k) * pairs + part)

    peers = [row_peer(k) for k in range(1, rows)]
    peers += [grp_peer(k) for k in range(1, rows)]
    peers += [part_peer(k) for k in range(1, pairs)]

    barrier = pltpu.get_barrier_semaphore()

    def greet(peer):
        pl.semaphore_signal(barrier, inc=1, device_id=peer, device_id_type=MESH)

    for k in range(1, rows):
        greet(pick_source(k))

    @pl.when(row != group)
    def _():
        greet(pick_source(0))

    for peer in peers:
        greet(peer)
    others = jnp.where(row != group, rows, rows - 1)
    tables = [
        pltpu.make_async_copy(up_hpos, up_pos, tab_sem.at[2]),
        pltpu.make_async_copy(dn_hpos, dn_pos, tab_sem.at[3]),
    ]
    for table in tables:
        table.start()

    mine = pl.ds(row * slots, slots)
    loads = [
        pltpu.make_async_copy(up_hbm, up_mat.at[mine], loc_sem.at[2]),
        pltpu.make_async_copy(dn_hbm, dn_mat.at[mine], loc_sem.at[3]),
    ]
    for load in loads:
        load.start()
    home = pl.ds(part * wide, wide)
    for a, (src, dst) in enumerate(((x_hbm, x_all), (y_hbm, y_all))):
        for t in range(chunks):
            for b in range(wide):
                pltpu.make_async_copy(
                    src.at[pl.ds(t * step, step), pl.ds(b * blk, blk)],
                    dst[t].at[part * wide + b], own_sem.at[a, t],
                ).start()
            loads.append(
                pltpu.make_async_copy(dst[t].at[home], dst[t].at[home], own_sem.at[a, t])
            )
    for table in tables:
        table.wait()
    lane = lax.broadcasted_iota(jnp.int32, (8, 128), 1)
    sub = lax.broadcasted_iota(jnp.int32, (8, 128), 0)
    packed = jnp.full((8, 128), -1, jnp.int32)
    for s in range(slots):
        for j, src in enumerate((up_pos, up_pos, dn_pos, dn_pos)):
            packed = jnp.where((sub == s) & (lane == j), src[s, j % 2], packed)
    own_pos[...] = packed
    row_pos[row] = packed

    pl.semaphore_wait(barrier, len(peers) + others)

    def pos_grp(k):
        return remote(
            own_pos, grp_pos.at[group], gp_send.at[k], gp_recv.at[group], pick_peer(k)
        )

    def pos_grp_in(k):
        whose = grp_of(k)
        return remote(
            own_pos, grp_pos.at[whose], gp_send.at[k], gp_recv.at[whose], pick_peer(k)
        )

    for k in range(1, rows):
        pos_grp(k).start()

    @pl.when(row != group)
    def _():
        pos_grp(0).start()

    @pl.when(row == group)
    def _():
        grp_pos[group] = packed

    pos_row = []
    for k in range(1, rows):
        copy = remote(own_pos, row_pos.at[row], rp_send.at[k], rp_recv.at[k], row_peer(k))
        copy.start()
        pos_row.append(copy)
    swap = {}
    for t in range(chunks):
        here = pl.ds(t * step, step)
        for a, (src, dst) in enumerate(((x_hbm, x_all), (y_hbm, y_all))):
            for k in range(1, pairs):
                sems = (ex_send.at[a, t, k], ex_recv.at[a, t, k], part_peer(k))
                for b in range(wide):
                    remote(
                        src.at[here, pl.ds(b * blk, blk)],
                        dst[t].at[part * wide + b], *sems,
                    ).start()
                swap[a, t, k] = remote(dst[t].at[home], dst[t].at[home], *sems)
    mats = []
    for a, (src, dst) in enumerate(((up_hbm, up_mat), (dn_hbm, dn_mat))):
        for k in range(1, rows):
            copy = remote(src, dst.at[mine], w_send.at[a, k], w_recv.at[a, k], row_peer(k))
            copy.start()
            mats.append(copy)

    for k in range(1, rows):
        pos_grp_in(k).wait_recv()

    @pl.when(row != group)
    def _():
        pos_grp_in(0).wait_recv()

    grp_copy = pltpu.make_async_copy(grp_pos, grp_tab, tab_sem.at[1])
    grp_copy.start()
    grp_copy.wait()
    for load in loads:
        load.wait()

    sel = {}
    for t in range(chunks):
        here = pl.ds(t * step, step)
        for a, (src, out, dst) in enumerate(((x_all, x_out, x_sel), (y_all, y_out, y_sel))):
            for k in range(1, pairs):
                swap[a, t, k].wait_recv()

            def pick(whose, s):
                return src[t][jnp.maximum(grp_tab[whose, s, 3 * a], 0)]

            for k in range(1, rows):
                for s in range(slots):
                    out[k, s, here] = pick(grp_of(k), s)
                copy = remote(
                    out.at[k, :, here], dst.at[pl.ds(group * slots, slots), here],
                    sel_send.at[a, t, k], sel_recv.at[a, t, k], grp_peer(k),
                )
                copy.start()
                sel[a, t, k] = copy
            for s in range(slots):
                dst[group * slots + s, here] = pick(group, s)

    for copy in pos_row:
        copy.wait()
    row_copy = pltpu.make_async_copy(row_pos, row_tab, tab_sem.at[0])
    row_copy.start()
    for copy in mats:
        copy.wait_recv()
    row_copy.wait()

    def up_col(i):
        return row_tab[i // slots, i % slots, 1]

    def down_row(i):
        return row_tab[i // slots, i % slots, 2]

    def gather_block(spot, t):
        here = pl.ds(t * step, step)
        summed = jnp.zeros((step, blk), jnp.float32)
        for j in range(total):
            keep = flag(grp_tab[j // slots, j % slots, 0] == spot)
            summed += keep * back_in[j, here].astype(jnp.float32)
        return summed

    back, fold = {}, {}

    def send_fold(t):
        here = pl.ds(t * step, step)
        for k in range(1, rows):
            back[t, k].wait_recv()
        for k in range(1, pairs):

            @pl.loop(0, wide)
            def _(b):
                lanes = pl.ds(pl.multiple_of(b * blk, blk), blk)
                value = gather_block(part_of(k) * wide + b, t)
                fold_out[k, here, lanes] = value.astype(jnp.bfloat16)

            copy = remote(
                fold_out.at[k, here], fold_in.at[k, here],
                fx_send.at[t, k], fx_recv.at[t, k], part_peer(k),
            )
            copy.start()
            fold[t, k] = copy

    def sum_home(t):
        @pl.loop(0, wide)
        def _(b):
            lanes = pl.ds(pl.multiple_of(b * blk, blk), blk)
            home_sum[pl.ds(t * step, step), lanes] = gather_block(part * wide + b, t)

    for t in range(chunks):
        here = pl.ds(t * step, step)
        for a in range(2):
            for k in range(1, rows):
                sel[a, t, k].wait_recv()

        @each(total)
        def _(i):
            block_out[i, here] = dot(x_sel[i, here], up_mat[i], 1, 0)
            down_part[i] = dot(y_sel[i, here], dn_mat[i], 1, 1)

        @each(total)
        def _(i):
            spot = up_col(i)
            hidden = jnp.zeros((step, blk), jnp.float32)
            grad = jnp.zeros((step, blk), jnp.float32)
            for j in range(total):
                hidden += flag((up_col(j) == spot) & (spot >= 0)) * block_out[j, here]
                grad += flag((down_row(j) == spot) & (spot >= 0)) * down_part[j]
            _, slope = gelu_parts(hidden)
            dh = (grad * slope).astype(jnp.bfloat16)
            dhid[i, here] = dh
            back_out[i, here] = dot(dh, up_mat[i], 1, 1).astype(jnp.bfloat16)

        for k in range(1, rows):
            copy = remote(
                back_out.at[pl.ds(grp_of(k) * slots, slots), here],
                back_in.at[pl.ds(group * slots, slots), here],
                bk_send.at[t, k], bk_recv.at[t, k], grp_peer(k),
            )
            copy.start()
            back[t, k] = copy
        for s in range(slots):
            back_in[group * slots + s, here] = back_out[group * slots + s, here]
        if t > 0:
            send_fold(t - 1)

    @each(total)
    def _(i):
        spot = down_row(i)
        hidden = jnp.zeros((tok, blk), jnp.float32)
        for j in range(total):
            hidden += flag((up_col(j) == spot) & (spot >= 0)) * block_out[j]
        value, _ = gelu_parts(hidden)
        act = value.astype(jnp.bfloat16)
        term = dot(act, y_sel[i], 0, 0) * flag(spot >= 0)
        dn_out[i] = term.astype(jnp.bfloat16)
        term = dot(x_sel[i], dhid[i], 0, 0) * flag(up_col(i) >= 0)
        up_out[i] = term.astype(jnp.bfloat16)

    grads = []
    for a, (src, dst) in enumerate(((up_out, up_in), (dn_out, dn_in))):
        for k in range(1, rows):
            copy = remote(
                src.at[pl.ds(lax.rem(row + k, rows) * slots, slots)], dst.at[k],
                gr_send.at[a, k], gr_recv.at[a, k], row_peer(k),
            )
            copy.start()
            grads.append(copy)

    send_fold(chunks - 1)
    for t in range(chunks):
        sum_home(t)

    for t in range(chunks):
        here = pl.ds(t * step, step)
        value = home_sum[here]
        for k in range(1, pairs):
            fold[t, k].wait_recv()
            value += fold_in[k, here].astype(jnp.float32)
        gin_ref[here] = value.astype(jnp.bfloat16)

    for copy in grads:
        copy.wait_recv()
    for src, got, dst in ((up_out, up_in, ugrad_ref), (dn_out, dn_in, dgrad_ref)):
        for s in range(slots):
            summed = src[row * slots + s].astype(jnp.float32)
            for k in range(1, rows):
                summed += got[k, s].astype(jnp.float32)
            dst[s] = summed.astype(jnp.bfloat16)

    for k in range(1, rows):
        pos_grp(k).wait_send()

    @pl.when(row != group)
    def _():
        pos_grp(0).wait_send()

    for group_of in (swap, sel, back, fold):
        for copy in group_of.values():
            copy.wait_send()
    for copy in mats + grads:
        copy.wait_send()


def body(rows, cols, inputs, grad_out, up_blocks, up_where, down_blocks, down_where):
    pairs = cols // rows
    slots, blk = up_blocks.shape[:2]
    tok, width = inputs.shape
    total = rows * slots
    chunks = CHUNKS
    bf, f32 = jnp.bfloat16, jnp.float32
    dma = pltpu.SemaphoreType.DMA
    vmem, smem = pltpu.VMEM, pltpu.SMEM
    step = tok // chunks
    scratch = [
        smem((slots, 2), jnp.int32),
        smem((slots, 2), jnp.int32),
        vmem((8, 128), jnp.int32),
        vmem((rows, 8, 128), jnp.int32),
        vmem((rows, 8, 128), jnp.int32),
        smem((rows, 8, 128), jnp.int32),
        smem((rows, 8, 128), jnp.int32),
        [vmem((pairs * width // blk, step, blk), bf) for _ in range(chunks)],
        [vmem((pairs * width // blk, step, blk), bf) for _ in range(chunks)],
        vmem((rows, slots, tok, blk), bf),
        vmem((rows, slots, tok, blk), bf),
        vmem((total, tok, blk), bf),
        vmem((total, tok, blk), bf),
        vmem((total, blk, blk), bf),
        vmem((total, blk, blk), bf),
        vmem((total, tok, blk), f32),
        vmem((total, step, blk), f32),
        vmem((tok, width), f32),
        vmem((total, tok, blk), bf),
        vmem((total, tok, blk), bf),
        vmem((total, tok, blk), bf),
        vmem((pairs, tok, width), bf),
        vmem((pairs, tok, width), bf),
        vmem((total, blk, blk), bf),
        vmem((rows, slots, blk, blk), bf),
        vmem((total, blk, blk), bf),
        vmem((rows, slots, blk, blk), bf),
        dma((4,)),
        dma((2, chunks)),
        dma((4,)),
    ]
    for shape in (
        (rows,), (rows,), (2, chunks, pairs), (2, rows),
        (2, chunks, rows), (chunks, rows), (chunks, pairs), (2, rows),
    ):
        scratch += [dma(shape), dma(shape)]
    hbm = pl.BlockSpec(memory_space=pl.ANY)
    full = pl.BlockSpec(memory_space=pltpu.VMEM)
    return pl.pallas_call(
        functools.partial(kernel, rows, pairs, slots, chunks),
        out_shape=(
            vmem(inputs.shape, bf),
            vmem(up_blocks.shape, bf),
            vmem(down_blocks.shape, bf),
        ),
        in_specs=[hbm] * 6,
        out_specs=(full, full, full),
        scratch_shapes=scratch,
        compiler_params=pltpu.CompilerParams(collective_id=0, has_side_effects=True),
    )(inputs, grad_out, up_blocks, down_blocks, up_where, down_where)


def solution(mesh):
    rows, cols = mesh.shape["row"], mesh.shape["col"]
    placed = (
        P("row", "col"),
        P("row", "col"),
        P("row", "col", None),
        P("row", "col"),
        P("row", "col", None),
        P("row", "col"),
    )
    return jax.shard_map(
        functools.partial(body, rows, cols),
        mesh=mesh,
        in_specs=placed,
        out_specs=(P("row", "col"), P("row", "col", None), P("row", "col", None)),
        check_vma=False,
    )
```

```python
import functools

import jax
import jax.numpy as jnp
from jax import lax
from jax.experimental import pallas as pl
from jax.experimental.pallas import tpu as pltpu
from jax.sharding import PartitionSpec as P

MESH = pl.DeviceIdType.MESH
CHUNKS = 2
PIECES = 2


def gelu_parts(hidden):
    cube = hidden * hidden * hidden
    inner = 0.7978845608028654 * (hidden + 0.044715 * cube)
    tanh_val = jnp.tanh(inner)
    value = 0.5 * hidden * (1.0 + tanh_val)
    slope = 0.5 * (1.0 + tanh_val) + 0.5 * hidden * (
        1.0 - tanh_val * tanh_val
    ) * 0.7978845608028654 * (1.0 + 0.134145 * hidden * hidden)
    return (value, slope)


def dot(left, right, left_dim, right_dim):
    return lax.dot_general(
        left, right, (((left_dim,), (right_dim,)), ((), ())),
        preferred_element_type=jnp.float32,
    )


def each(count, unroll=8):
    size = max(n for n in range(1, unroll + 1) if count % n == 0)

    def run(body):
        if size == count:
            for i in range(count):
                body(i)
            return

        @pl.loop(0, count // size)
        def _(outer):
            for i in range(size):
                body(outer * size + i)

    return run


def flag(pred):
    return pred.astype(jnp.float32)


def kernel(
    rows, pairs, slots, chunks, pieces,
    x_hbm, y_hbm, up_hbm, dn_hbm, up_hpos, dn_hpos,
    gin_ref, ugrad_ref, dgrad_ref,
    up_pos, dn_pos, own_pos, row_pos, grp_pos, row_tab, grp_tab,
    x_all, y_all, x_out, y_out, x_sel, y_sel,
    up_mat, dn_mat, block_out, down_part, slope_at, home_sum, act, dhid,
    back_out, back_in, fold_out, fold_in,
    up_out, up_in, dn_out, dn_in,
    loc_sem, own_sem, tab_sem,
    rp_send, rp_recv, gp_send, gp_recv, ex_send, ex_recv, w_send, w_recv,
    sel_send, sel_recv, bk_send, bk_recv, fx_send, fx_recv, gr_send, gr_recv,
):
    row = lax.axis_index("row")
    col = lax.axis_index("col")
    group, part = col // pairs, col % pairs
    tok = x_hbm.shape[0]
    blk = up_hbm.shape[1]
    wide = x_hbm.shape[1] // blk
    step = tok // chunks
    part_step = step // pieces
    total = rows * slots

    def row_peer(k):
        return (lax.rem(row + k, rows), col)

    def grp_of(k):
        return lax.rem(group + k, rows)

    def grp_peer(k):
        return (row, grp_of(k) * pairs + part)

    def part_of(k):
        return lax.rem(part + k, pairs)

    def part_peer(k):
        return (row, group * pairs + part_of(k))

    def remote(src, dst, send, recv, peer):
        return pltpu.make_async_remote_copy(
            src_ref=src, dst_ref=dst, send_sem=send, recv_sem=recv,
            device_id=peer, device_id_type=MESH,
        )

    def pick_peer(k):
        return (lax.rem(row + k, rows), row * pairs + part)

    def pick_source(k):
        return (group, grp_of(k) * pairs + part)

    peers = [row_peer(k) for k in range(1, rows)]
    peers += [grp_peer(k) for k in range(1, rows)]
    peers += [part_peer(k) for k in range(1, pairs)]

    barrier = pltpu.get_barrier_semaphore()

    def greet(peer):
        pl.semaphore_signal(barrier, inc=1, device_id=peer, device_id_type=MESH)

    for k in range(1, rows):
        greet(pick_source(k))

    @pl.when(row != group)
    def _():
        greet(pick_source(0))

    for peer in peers:
        greet(peer)
    others = jnp.where(row != group, rows, rows - 1)
    tables = [
        pltpu.make_async_copy(up_hpos, up_pos, tab_sem.at[2]),
        pltpu.make_async_copy(dn_hpos, dn_pos, tab_sem.at[3]),
    ]
    for table in tables:
        table.start()

    mine = pl.ds(row * slots, slots)
    loads = [
        pltpu.make_async_copy(up_hbm, up_mat.at[mine], loc_sem.at[2]),
        pltpu.make_async_copy(dn_hbm, dn_mat.at[mine], loc_sem.at[3]),
    ]
    for load in loads:
        load.start()
    home = pl.ds(part * wide, wide)
    for a, (src, dst) in enumerate(((x_hbm, x_all), (y_hbm, y_all))):
        for t in range(chunks):
            for b in range(wide):
                pltpu.make_async_copy(
                    src.at[pl.ds(t * step, step), pl.ds(b * blk, blk)],
                    dst[t].at[part * wide + b], own_sem.at[a, t],
                ).start()
            loads.append(
                pltpu.make_async_copy(dst[t].at[home], dst[t].at[home], own_sem.at[a, t])
            )
    for table in tables:
        table.wait()
    lane = lax.broadcasted_iota(jnp.int32, (8, 128), 1)
    sub = lax.broadcasted_iota(jnp.int32, (8, 128), 0)
    packed = jnp.full((8, 128), -1, jnp.int32)
    for s in range(slots):
        for j, src in enumerate((up_pos, up_pos, dn_pos, dn_pos)):
            packed = jnp.where((sub == s) & (lane == j), src[s, j % 2], packed)
    own_pos[...] = packed
    row_pos[row] = packed

    pl.semaphore_wait(barrier, len(peers) + others)

    def pos_grp(k):
        return remote(
            own_pos, grp_pos.at[group], gp_send.at[k], gp_recv.at[group], pick_peer(k)
        )

    def pos_grp_in(k):
        whose = grp_of(k)
        return remote(
            own_pos, grp_pos.at[whose], gp_send.at[k], gp_recv.at[whose], pick_peer(k)
        )

    for k in range(1, rows):
        pos_grp(k).start()

    @pl.when(row != group)
    def _():
        pos_grp(0).start()

    @pl.when(row == group)
    def _():
        grp_pos[group] = packed

    pos_row = []
    for k in range(1, rows):
        copy = remote(own_pos, row_pos.at[row], rp_send.at[k], rp_recv.at[k], row_peer(k))
        copy.start()
        pos_row.append(copy)
    swap = {}
    for t in range(chunks):
        here = pl.ds(t * step, step)
        for a, (src, dst) in enumerate(((x_hbm, x_all), (y_hbm, y_all))):
            for k in range(1, pairs):
                sems = (ex_send.at[a, t, k], ex_recv.at[a, t, k], part_peer(k))
                for b in range(wide):
                    remote(
                        src.at[here, pl.ds(b * blk, blk)],
                        dst[t].at[part * wide + b], *sems,
                    ).start()
                swap[a, t, k] = remote(dst[t].at[home], dst[t].at[home], *sems)
    mats = []
    for a, (src, dst) in enumerate(((up_hbm, up_mat), (dn_hbm, dn_mat))):
        for k in range(1, rows):
            copy = remote(src, dst.at[mine], w_send.at[a, k], w_recv.at[a, k], row_peer(k))
            copy.start()
            mats.append(copy)

    for k in range(1, rows):
        pos_grp_in(k).wait_recv()

    @pl.when(row != group)
    def _():
        pos_grp_in(0).wait_recv()

    grp_copy = pltpu.make_async_copy(grp_pos, grp_tab, tab_sem.at[1])
    grp_copy.start()
    grp_copy.wait()
    for load in loads:
        load.wait()

    sel = {}

    def pick_send(t, a):
        here = pl.ds(t * step, step)
        src, out, dst = ((x_all, x_out, x_sel), (y_all, y_out, y_sel))[a]
        for k in range(1, pairs):
            swap[a, t, k].wait_recv()

        def pick(whose, s):
            return src[t][jnp.maximum(grp_tab[whose, s, 3 * a], 0)]

        for k in range(1, rows):
            for s in range(slots):
                out[k, s, here] = pick(grp_of(k), s)
            copy = remote(
                out.at[k, :, here], dst.at[pl.ds(group * slots, slots), here],
                sel_send.at[a, t, k], sel_recv.at[a, t, k], grp_peer(k),
            )
            copy.start()
            sel[a, t, k] = copy
        for s in range(slots):
            dst[group * slots + s, here] = pick(group, s)

    def wait_mats():
        for copy in pos_row:
            copy.wait()
        row_copy = pltpu.make_async_copy(row_pos, row_tab, tab_sem.at[0])
        row_copy.start()
        for copy in mats:
            copy.wait_recv()
        row_copy.wait()

    def up_col(i):
        return row_tab[i // slots, i % slots, 1]

    def down_row(i):
        return row_tab[i // slots, i % slots, 2]

    def rows_of(piece):
        return pl.ds(piece * part_step, part_step)

    def gather_block(spot, piece):
        summed = jnp.zeros((part_step, blk), jnp.float32)
        for j in range(total):
            keep = flag(grp_tab[j // slots, j % slots, 0] == spot)
            summed += keep * back_in[j, rows_of(piece)].astype(jnp.float32)
        return summed

    back, fold, grads = {}, {}, []

    def send_fold(piece):
        here = rows_of(piece)
        for k in range(1, rows):
            back[piece, k].wait_recv()
        for k in range(1, pairs):

            @pl.loop(0, wide)
            def _(b):
                lanes = pl.ds(pl.multiple_of(b * blk, blk), blk)
                value = gather_block(part_of(k) * wide + b, piece)
                fold_out[k, here, lanes] = value.astype(jnp.bfloat16)

            copy = remote(
                fold_out.at[k, here], fold_in.at[k, here],
                fx_send.at[piece, k], fx_recv.at[piece, k], part_peer(k),
            )
            copy.start()
            fold[piece, k] = copy

    def forward(t):
        here = pl.ds(t * step, step)
        for k in range(1, rows):
            sel[0, t, k].wait_recv()

        @each(total)
        def _(i):
            block_out[i] = dot(x_sel[i, here], up_mat[i], 1, 0)

        @each(total)
        def _(i):
            spot, other = up_col(i), down_row(i)
            hidden = jnp.zeros((step, blk), jnp.float32)
            taken = jnp.zeros((step, blk), jnp.float32)
            for j in range(total):
                block = block_out[j]
                hidden += flag((up_col(j) == spot) & (spot >= 0)) * block
                taken += flag((up_col(j) == other) & (other >= 0)) * block
            slope_at[i, here] = gelu_parts(hidden)[1]
            act[i, here] = gelu_parts(taken)[0].astype(jnp.bfloat16)

    def backward(t):
        here = pl.ds(t * step, step)
        for k in range(1, rows):
            sel[1, t, k].wait_recv()

        @each(total)
        def _(i):
            down_part[i] = dot(y_sel[i, here], dn_mat[i], 1, 1)

        @each(total)
        def _(i):
            spot = up_col(i)
            grad = jnp.zeros((step, blk), jnp.float32)
            for j in range(total):
                grad += flag((down_row(j) == spot) & (spot >= 0)) * down_part[j]
            dh = (grad * slope_at[i, here]).astype(jnp.bfloat16)
            dhid[i, here] = dh
            back_out[i, here] = dot(dh, up_mat[i], 1, 1).astype(jnp.bfloat16)

        for piece in range(t * pieces, (t + 1) * pieces):
            for k in range(1, rows):
                copy = remote(
                    back_out.at[pl.ds(grp_of(k) * slots, slots), rows_of(piece)],
                    back_in.at[pl.ds(group * slots, slots), rows_of(piece)],
                    bk_send.at[piece, k], bk_recv.at[piece, k], grp_peer(k),
                )
                copy.start()
                back[piece, k] = copy
        for s in range(slots):
            back_in[group * slots + s, here] = back_out[group * slots + s, here]

    def send_grads(a, src, dst):
        for k in range(1, rows):
            copy = remote(
                src.at[pl.ds(lax.rem(row + k, rows) * slots, slots)], dst.at[k],
                gr_send.at[a, k], gr_recv.at[a, k], row_peer(k),
            )
            copy.start()
            grads.append(copy)

    for t in range(chunks - 1):
        pick_send(t, 0)
        pick_send(t, 1)
    pick_send(chunks - 1, 0)
    wait_mats()
    forward(0)
    pick_send(chunks - 1, 1)
    for t in range(chunks):
        if t > 0:
            forward(t)
        backward(t)

    @each(total)
    def _(i):
        term = dot(act[i], y_sel[i], 0, 0) * flag(down_row(i) >= 0)
        dn_out[i] = term.astype(jnp.bfloat16)

    send_grads(1, dn_out, dn_in)

    @each(total)
    def _(i):
        term = dot(x_sel[i], dhid[i], 0, 0) * flag(up_col(i) >= 0)
        up_out[i] = term.astype(jnp.bfloat16)

    send_grads(0, up_out, up_in)

    for piece in range(chunks * pieces):
        send_fold(piece)
    for piece in range(chunks * pieces):

        @pl.loop(0, wide)
        def _(b):
            lanes = pl.ds(pl.multiple_of(b * blk, blk), blk)
            home_sum[rows_of(piece), lanes] = gather_block(part * wide + b, piece)

    for piece in range(chunks * pieces):
        here = rows_of(piece)
        value = home_sum[here]
        for k in range(1, pairs):
            fold[piece, k].wait_recv()
            value += fold_in[k, here].astype(jnp.float32)
        gin_ref[here] = value.astype(jnp.bfloat16)

    for copy in grads:
        copy.wait_recv()
    for src, got, dst in ((up_out, up_in, ugrad_ref), (dn_out, dn_in, dgrad_ref)):
        for s in range(slots):
            summed = src[row * slots + s].astype(jnp.float32)
            for k in range(1, rows):
                summed += got[k, s].astype(jnp.float32)
            dst[s] = summed.astype(jnp.bfloat16)

    for k in range(1, rows):
        pos_grp(k).wait_send()

    @pl.when(row != group)
    def _():
        pos_grp(0).wait_send()

    for group_of in (swap, sel, back, fold):
        for copy in group_of.values():
            copy.wait_send()
    for copy in mats + grads:
        copy.wait_send()


def body(rows, cols, inputs, grad_out, up_blocks, up_where, down_blocks, down_where):
    pairs = cols // rows
    slots, blk = up_blocks.shape[:2]
    tok, width = inputs.shape
    total = rows * slots
    chunks, pieces = CHUNKS, PIECES
    bf, f32 = jnp.bfloat16, jnp.float32
    dma = pltpu.SemaphoreType.DMA
    vmem, smem = pltpu.VMEM, pltpu.SMEM
    step = tok // chunks
    scratch = [
        smem((slots, 2), jnp.int32),
        smem((slots, 2), jnp.int32),
        vmem((8, 128), jnp.int32),
        vmem((rows, 8, 128), jnp.int32),
        vmem((rows, 8, 128), jnp.int32),
        smem((rows, 8, 128), jnp.int32),
        smem((rows, 8, 128), jnp.int32),
        [vmem((pairs * width // blk, step, blk), bf) for _ in range(chunks)],
        [vmem((pairs * width // blk, step, blk), bf) for _ in range(chunks)],
        vmem((rows, slots, tok, blk), bf),
        vmem((rows, slots, tok, blk), bf),
        vmem((total, tok, blk), bf),
        vmem((total, tok, blk), bf),
        vmem((total, blk, blk), bf),
        vmem((total, blk, blk), bf),
        vmem((total, step, blk), f32),
        vmem((total, step, blk), f32),
        vmem((total, tok, blk), f32),
        vmem((tok, width), f32),
        vmem((total, tok, blk), bf),
        vmem((total, tok, blk), bf),
        vmem((total, tok, blk), bf),
        vmem((total, tok, blk), bf),
        vmem((pairs, tok, width), bf),
        vmem((pairs, tok, width), bf),
        vmem((total, blk, blk), bf),
        vmem((rows, slots, blk, blk), bf),
        vmem((total, blk, blk), bf),
        vmem((rows, slots, blk, blk), bf),
        dma((4,)),
        dma((2, chunks)),
        dma((4,)),
    ]
    for shape in (
        (rows,), (rows,), (2, chunks, pairs), (2, rows),
        (2, chunks, rows), (chunks * pieces, rows), (chunks * pieces, pairs), (2, rows),
    ):
        scratch += [dma(shape), dma(shape)]
    hbm = pl.BlockSpec(memory_space=pl.ANY)
    full = pl.BlockSpec(memory_space=pltpu.VMEM)
    return pl.pallas_call(
        functools.partial(kernel, rows, pairs, slots, chunks, pieces),
        out_shape=(
            vmem(inputs.shape, bf),
            vmem(up_blocks.shape, bf),
            vmem(down_blocks.shape, bf),
        ),
        in_specs=[hbm] * 6,
        out_specs=(full, full, full),
        scratch_shapes=scratch,
        compiler_params=pltpu.CompilerParams(collective_id=0, has_side_effects=True),
    )(inputs, grad_out, up_blocks, down_blocks, up_where, down_where)


def solution(mesh):
    rows, cols = mesh.shape["row"], mesh.shape["col"]
    placed = (
        P("row", "col"),
        P("row", "col"),
        P("row", "col", None),
        P("row", "col"),
        P("row", "col", None),
        P("row", "col"),
    )
    return jax.shard_map(
        functools.partial(body, rows, cols),
        mesh=mesh,
        in_specs=placed,
        out_specs=(P("row", "col"), P("row", "col", None), P("row", "col", None)),
        check_vma=False,
    )
```
